128 devices in a mesh: energy: 8 (over x, y_lo), row: 4 (over z), col: 4 (over y_hi, core).
Axes of the slice: x: 4, y: 4 (y_hi: 2, y_lo: 2; y = y_hi * 2 + y_lo), z: 4, core: 2. Of those that a mesh axis runs over, the one named last changes fastest.
Arguments:
- object_field: float32 [2, 32, 1024, 1024], P(None, 'energy', 'row', 'col'), may hold values from -6 to 6
- probe_field: float32 [2, 32, 256, 256], P(None, 'energy'), may hold values from -5 to 5
- amplitudes: float32 [32, 4, 4, 4, 256, 256], P('energy', 'row', 'col'), may hold values from 0 to 3
- kk_kernel: float32 [2, 2, 32, 32], replicated, may hold values from -0.75 to 0.75
- offsets: int32 [4, 4, 4, 2], P('row', 'col'), may hold values from 0 to 128, as said below
Outputs:
- blended: float32 [2, 32, 1024, 1024], P(None, 'energy', 'row', 'col')
- new_probe: float32 [2, 32, 256, 256], P(None, 'energy')
The draws below stay inside these ranges and needn't reach their ends.
Inputs may be any that keep to these rules, and one draw needn't show every extreme that they name: `offsets`: position k of every tile starts within 32 of 0 for k = 0, 1 and within 32 below 128 for k = 2, 3 in rows; in columns likewise, near 0 for even k and near the top for odd k.
All inputs are finite; a program needn't handle non-finite values.
Results may differ from the reference program's by a relative error of at most 0.0001.
Values sent between devices are 32-bit elements; how exact they have to be, the bound alone decides.
A program may use at most 128 MiB of HBM per device.

```python
import math
import jax
import jax.numpy as jnp
from jax import lax

E = 32
WIN = 256
TILE = 256
HALO = 64
JITTER = 32
TR = 4
TC = 4
NY = 1024
NX = 1024


def draw_offsets(key, part):
    jitter = jax.random.randint(key, (TR, TC, 4, 2), 0, JITTER + 1, dtype=jnp.int32)
    jitter = jitter.at[0, 0, 0, :].set(0).at[0, 0, 3, :].set(0)
    position = jnp.arange(4, dtype=jnp.int32)
    far_side = jnp.stack([position >= 2, position % 2 == 1], axis=1)
    reach = TILE + 2 * HALO - WIN
    return jnp.where(far_side[None, None], reach - jitter, jitter).astype(jnp.int32)


def block_scale(key, dims, cuts, least, top_value):
    def one(dim, shards_of):
        steps = jax.random.uniform(jax.random.fold_in(jax.random.fold_in(key, 6), dim), (shards_of,), jnp.float32, least / len(cuts), top_value / len(cuts))
        return jnp.repeat(jnp.exp(steps), dims[dim] // shards_of).reshape((-1,) + (1,) * (len(dims) - dim - 1))

    level = one(*cuts[0])
    for cut in cuts[1:]:
        level = level * one(*cut)
    return level


def centred(stream_key, shape, width, limit, shards=(), kind=jnp.bfloat16):
    factor_of = block_scale(stream_key, shape, shards, -0.22, 0.18) if shards else 1.0
    entries = jax.random.normal(stream_key, shape, jnp.float32) * width * factor_of
    return jnp.minimum(jnp.maximum(entries, -limit), limit).astype(kind)


def setup_inputs(seed: int = 0) -> dict:
    key_list = jax.random.split(jax.random.key(seed), 6)
    object_field = centred(key_list[0], (2, E, NY, NX), 1.0, 6.0, ((1, 8), (2, 4), (3, 4)), jnp.float32)
    probe_field = centred(key_list[1], (2, E, WIN, WIN), 0.7, 5.0, ((1, 8),), jnp.float32)
    amplitudes = jnp.clip(3.0 * jax.random.uniform(key_list[2], (E, TR, TC, 4, WIN, WIN), jnp.float32) ** block_scale(key_list[2], (E, TR, TC, 4, WIN, WIN), ((0, 8), (1, 4), (2, 4)), -0.2, 0.2), 0.0, 3.0)
    kk_kernel = centred(key_list[3], (2, 2, E, E), (2 * E) ** -0.5, 0.75, (), jnp.float32)
    offsets = draw_offsets(jax.random.fold_in(key_list[5], 71), 0)
    return {"object_field": object_field, "probe_field": probe_field, "amplitudes": amplitudes, "kk_kernel": kk_kernel, "offsets": offsets}


PRECISE = lax.Precision.HIGHEST
STEP = 0.25
PROBE_STEP = 0.5
FLOOR = 0.25

def dft_tables(length):
    counter = jnp.arange(length, dtype=jnp.int32)
    phases = counter[:, None] * counter[None, :] % length
    angles = phases.astype(jnp.float32) * (2.0 * math.pi / length)
    factor = 1.0 / math.sqrt(length)
    return (jnp.cos(angles) * factor, -jnp.sin(angles) * factor)

def left_product(cos_table, sin_table, real_part, imag_part):

    def multiply(matrix, field):
        return jnp.einsum('uv,evw->euw', matrix, field, precision=PRECISE)
    return (multiply(cos_table, real_part) - multiply(sin_table, imag_part), multiply(cos_table, imag_part) + multiply(sin_table, real_part))

def right_product(cos_table, sin_table, real_part, imag_part):

    def multiply(field, matrix):
        return jnp.einsum('euv,vw->euw', field, matrix, precision=PRECISE)
    return (multiply(real_part, cos_table) - multiply(imag_part, sin_table), multiply(real_part, sin_table) + multiply(imag_part, cos_table))

def transform(cos_table, sin_table, real_part, imag_part):
    real_part, imag_part = left_product(cos_table, sin_table, real_part, imag_part)
    return right_product(cos_table, sin_table, real_part, imag_part)

def position_update(window, probe_field, measured, cos_table, sin_table):
    probe_real, probe_imag = (probe_field[0], probe_field[1])
    window_real, window_imag = (window[0], window[1])
    exit_real = probe_real * window_real - probe_imag * window_imag
    exit_imag = probe_real * window_imag + probe_imag * window_real
    far_real, far_imag = transform(cos_table, sin_table, exit_real, exit_imag)
    modulus = jnp.sqrt(far_real * far_real + far_imag * far_imag)
    rescale = measured / jnp.maximum(modulus, FLOOR)
    back_real, back_imag = transform(cos_table, -sin_table, far_real * rescale, far_imag * rescale)
    diff_real = exit_real - back_real
    diff_imag = exit_imag - back_imag
    object_step = jnp.stack([probe_real * diff_real + probe_imag * diff_imag, probe_real * diff_imag - probe_imag * diff_real])
    probe_step = jnp.stack([window_real * diff_real + window_imag * diff_imag, window_real * diff_imag - window_imag * diff_real])
    return (object_step, probe_step)

def reference(object_field, probe_field, amplitudes, kk_kernel, offsets):
    cos_table, sin_table = dft_tables(WIN)
    padded = jnp.pad(object_field, ((0, 0), (0, 0), (HALO, HALO), (HALO, HALO)))
    anchor = jnp.zeros((), jnp.int32)
    shape = (2, E, WIN, WIN)

    def tile_step(tile_number, running):
        gradient, probe_grad = running
        tile_number = jnp.asarray(tile_number).astype(jnp.int32)
        row_tile = tile_number // TC
        col_tile = tile_number % TC
        for position in range(4):
            row_start = (row_tile * TILE + offsets[row_tile, col_tile, position, 0]).astype(jnp.int32)
            col_start = (col_tile * TILE + offsets[row_tile, col_tile, position, 1]).astype(jnp.int32)
            corner = (anchor, anchor, row_start, col_start)
            window = lax.dynamic_slice(padded, corner, shape)
            measured = amplitudes[:, row_tile, col_tile, position]
            object_step, probe_step = position_update(window, probe_field, measured, cos_table, sin_table)
            current = lax.dynamic_slice(gradient, corner, shape)
            gradient = lax.dynamic_update_slice(gradient, current + object_step, corner)
            probe_grad = probe_grad + probe_step
        return (gradient, probe_grad)
    start_state = (jnp.zeros_like(padded), jnp.zeros_like(probe_field))
    gradient, probe_grad = lax.fori_loop(0, TR * TC, tile_step, start_state)
    interior = gradient[:, :, HALO:HALO + NY, HALO:HALO + NX]
    stepped = object_field - STEP * interior
    new_probe = probe_field - PROBE_STEP / (4 * TR * TC) * probe_grad
    blended = stepped + jnp.einsum('abef,bfyx->aeyx', kk_kernel, stepped, precision=PRECISE)
    return (blended, new_probe)
```

```python
import functools

import jax
import jax.numpy as jnp
import numpy as np
from jax import lax
from jax.experimental import pallas as pl
from jax.experimental.pallas import tpu as pltpu
from jax.sharding import PartitionSpec as P

H = 128
N = 256
HALO = 64
STEP = 0.25
PROBE_STEP = 0.5
FLOOR = 0.25
F32 = jnp.float32
BF = jnp.bfloat16
MESH = pl.DeviceIdType.MESH
SIDES = ((-1, 0), (1, 0), (0, -1), (0, 1), (-1, -1), (-1, 1), (1, -1), (1, 1))


def tables():
    n = np.arange(H)[:, None].astype(np.float64)
    k = np.arange(H)[None, :].astype(np.float64)
    out = []
    for odd in (0, 1):
        angle = -2.0 * np.pi * ((n * (2 * k + odd)) % N) / N
        re, im = np.cos(angle) / 16.0, np.sin(angle) / 16.0
        out.append(np.block([[re, im], [-im, re]]))
    right = np.stack(out)
    both = np.stack([right, np.swapaxes(right, 1, 2)])
    hi = both.astype(np.float32).astype(jnp.bfloat16)
    lo = (both - hi.astype(np.float64)).astype(np.float32).astype(jnp.bfloat16)
    order = np.zeros((N, N), np.float32)
    for lane in range(H):
        order[2 * lane, lane] = 1
        order[2 * lane + 1, H + lane] = 1
    return np.stack([hi, lo], axis=2), order.astype(jnp.bfloat16)


def split(x):
    hi = x.astype(BF)
    return hi, (x - hi.astype(F32)).astype(BF)


def dot(a, b):
    return jnp.dot(a, b, preferred_element_type=F32)


def times_table(q, tab, side, odd):
    hi, lo = tab[side, odd, 0], tab[side, odd, 1]
    return dot(
        jnp.concatenate([q[...], q[:, :N]], axis=1), jnp.concatenate([hi, hi, lo], axis=0)
    )


def table_times(tab, side, odd, q):
    hi, lo = tab[side, odd, 0], tab[side, odd, 1]
    return dot(
        jnp.concatenate([hi, hi, lo], axis=1), jnp.concatenate([q[...], q[:N, :]], axis=0)
    )


def position(k, a, b, ext, probe, amp, grad, pg, tab, order, win, exi, ra, rb, la, lb, ap, asc, opad):
    base = lax.rem(k, 2)
    s = b + HALO - H * base
    rows_at = 64
    lane = lax.broadcasted_iota(jnp.int32, (rows_at, H), 1)
    keep = lane < H - s
    for rc in range(0, N, rows_at):
        rows = pl.ds(rc, rows_at)
        w = []
        for c in (0, 1):
            t = [pltpu.roll(ext[c, base + j, pl.ds(a + rc, rows_at), :], H - s, 1) for j in range(3)]
            w.append([jnp.where(keep, t[j], t[j + 1]) for j in (0, 1)])
        x = [[None, None], [None, None]]
        for j in (0, 1):
            cols = pl.ds(j * H, H)
            pr, pi = probe[0, rows, cols], probe[1, rows, cols]
            wr, wi = w[0][j], w[1][j]
            win[0, rows, cols] = wr
            win[1, rows, cols] = wi
            x[0][j] = pr * wr - pi * wi
            x[1][j] = pr * wi + pi * wr
            exi[0, rows, cols] = x[0][j]
            exi[1, rows, cols] = x[1][j]
        for c in (0, 1):
            for q, v in ((ra, x[c][0] + x[c][1]), (rb, x[c][0] - x[c][1])):
                hi, lo = split(v)
                q[rows, pl.ds(c * H, H)] = hi
                q[rows, pl.ds(N + c * H, H)] = lo
        hi, lo = split(amp[rows, :])
        ap[rows, pl.ds(0, N)] = hi
        ap[rows, pl.ds(N, N)] = lo
    y = [times_table(ra, tab, 0, 0), times_table(rb, tab, 0, 1)]
    for pc in (0, 1):
        cols = pl.ds(pc * H, H)
        for c in (0, 1):
            t = y[pc][:H, c * H:(c + 1) * H]
            u = y[pc][H:, c * H:(c + 1) * H]
            for q, v in ((la, t + u), (lb, t - u)):
                hi, lo = split(v)
                q[pl.ds(c * H, H), cols] = hi
                q[pl.ds(N + c * H, H), cols] = lo
    amps = dot(ap[...], jnp.concatenate([order[...], order[...]], axis=0))
    asc[0] = amps[:, :H]
    asc[1] = amps[:, H:]
    z = [table_times(tab, 1, 0, la), table_times(tab, 1, 1, lb)]
    for pr, q in ((0, la), (1, lb)):
        fr, fi = z[pr][:H], z[pr][H:]
        measured = jnp.concatenate([asc[j, pl.ds(pr, H, stride=2), :] for j in (0, 1)], axis=1)
        scale = measured * lax.rsqrt(jnp.maximum(fr * fr + fi * fi, FLOOR * FLOOR))
        for c, v in ((0, fr * scale), (1, fi * scale)):
            hi, lo = split(v)
            q[pl.ds(c * H, H), :] = hi
            q[pl.ds(N + c * H, H), :] = lo
    p, q = table_times(tab, 0, 0, la), table_times(tab, 0, 1, lb)
    for half, v in ((0, p + q), (1, p - q)):
        rows = pl.ds(half * H, H)
        for pc, dst in ((0, ra), (1, rb)):
            for c in (0, 1):
                hi, lo = split(v[c * H:(c + 1) * H, pc * H:(pc + 1) * H])
                dst[rows, pl.ds(c * H, H)] = hi
                dst[rows, pl.ds(N + c * H, H)] = lo
    p, q = times_table(ra, tab, 1, 0), times_table(rb, tab, 1, 1)
    back = (p + q, p - q)
    turned = lane >= s
    for rc in range(0, N, rows_at):
        rows = pl.ds(rc, rows_at)
        step = [[None] * 2, [None] * 2]
        for j in (0, 1):
            cols = pl.ds(j * H, H)
            dr = exi[0, rows, cols] - back[j][rc:rc + rows_at, :H]
            di = exi[1, rows, cols] - back[j][rc:rc + rows_at, H:]
            pr, pi = probe[0, rows, cols], probe[1, rows, cols]
            wr, wi = win[0, rows, cols], win[1, rows, cols]
            pg[0, rows, cols] += wr * dr + wi * di
            pg[1, rows, cols] += wr * di - wi * dr
            step[0][j] = pltpu.roll(pr * dr + pi * di, s, 1)
            step[1][j] = pltpu.roll(pr * di - pi * dr, s, 1)
        for c in (0, 1):
            at = pl.ds(32 + rc, rows_at)
            opad[c, 0, at, :] = jnp.where(turned, step[c][0], 0.0)
            opad[c, 1, at, :] = jnp.where(turned, step[c][1], step[c][0])
            opad[c, 2, at, :] = jnp.where(turned, 0.0, step[c][1])
    first = 96 * lax.div(k, 2)
    start = 32 - jnp.clip(a - first, 0, 32)
    for c in (0, 1):
        for j in range(3):
            for rc in range(0, 288, 32):
                at = pl.ds(pl.multiple_of(first + rc, 32), 32)
                grad[c, base + j, at, :] += opad[c, j, pl.ds(start + rc, 32), :]


def expand_kernel(kk, kx):
    out_row = lax.broadcasted_iota(jnp.int32, (512, 32), 0)
    out_col = lax.broadcasted_iota(jnp.int32, (512, 32), 1)
    out_energy = 4 * (out_row >> 6) + ((out_row >> 3) & 3)
    in_row = lax.broadcasted_iota(jnp.int32, (32, 512), 0)
    in_col = lax.broadcasted_iota(jnp.int32, (32, 512), 1)
    in_energy = 4 * ((in_col >> 4) & 7) + (in_col >> 7)
    r = lax.broadcasted_iota(jnp.int32, (512, 512), 0)
    c = lax.broadcasted_iota(jnp.int32, (512, 512), 1)
    same = (r & 7) == (c & 7)
    one = lambda m: jnp.where(m, 1.0, 0.0).astype(BF)
    pick = [one((in_energy == in_row) & (((in_col >> 3) & 1) == b)) for b in (0, 1)]
    place = [one((out_energy == out_col) & (((out_row >> 5) & 1) == a)) for a in (0, 1)]
    parts = [[split(kk[a, b]) for b in (0, 1)] for a in (0, 1)]
    for which in (0, 1):
        total = None
        for a in (0, 1):
            row = dot(parts[a][0][which], pick[0]) + dot(parts[a][1][which], pick[1])
            term = dot(place[a], row.astype(BF))
            total = term if total is None else total + term
        kx[which] = jnp.where(same, total, 0.0).astype(BF)


def kernel(
    offs, obj_any, probe_any, amp_any, kk, tab_any, order_any,
    blended_any, new_probe_any,
    obj, probe, amp, tab, order, kx,
    halo_rows, halo_cols, halo_corners, cols_out, corners_out,
    gr_in, gc_in, gk_in, gr_out, gc_out, gk_out,
    ext, grad, stepped, gathered, acc, coupled, returned,
    pg, core_in, row_in, far_in, total,
    win, exi, ra, rb, la, lb, ap, asc, opad,
    load_sem, halo_send, halo_recv, grad_send, grad_recv,
    in_send, in_recv, out_send, out_recv,
    p_send, p_recv, store_sem,
):
    me = lax.axis_index("energy")
    row = lax.axis_index("row")
    col = lax.axis_index("col")
    rows, cols = lax.axis_size("row"), lax.axis_size("col")
    core = lax.rem(col, 2)
    partner = {"col": col + 1 - 2 * core}
    high = lax.div(col, 2)
    across = {"col": col + 2 - 4 * high}

    def peer(slot):
        dx, dy = slot // 2, slot % 2
        x, y = lax.div(me, 2), lax.rem(me, 2)
        y2 = y + dy * (1 - 2 * y)
        return lax.rem(x + dx, 4) * 2 + y2, lax.rem(x + 4 - dx, 4) * 2 + y2

    def inside(dr, dc):
        ok = None
        for d, at, n in ((dr, row, rows), (dc, col, cols)):
            if d:
                here = at > 0 if d < 0 else at < n - 1
                ok = here if ok is None else ok & here
        return ok

    loads = []
    for e in range(4):
        loads.append(pltpu.make_async_copy(obj_any.at[:, e], obj.at[e], load_sem.at[e]))
    loads.append(pltpu.make_async_copy(probe_any, probe, load_sem.at[4]))
    loads.append(pltpu.make_async_copy(tab_any, tab, load_sem.at[5]))
    loads.append(pltpu.make_async_copy(order_any, order, load_sem.at[6]))
    for e in range(4):
        loads.append(pltpu.make_async_copy(amp_any.at[e, 0, 0], amp.at[e], load_sem.at[7 + e]))
    for copy in loads:
        copy.start()

    barrier = pltpu.get_barrier_semaphore()

    def greet(device):
        pl.semaphore_signal(barrier, inc=1, device_id=device, device_id_type=MESH)

    for dr, dc in SIDES:
        @pl.when(inside(dr, dc))
        def _():
            greet({"row": row + dr, "col": col + dc})
    for slot in range(1, 8):
        greet({"energy": peer(slot)[0]})
    for d in range(1, 4):
        r2 = lax.rem(row + d, rows)

        @pl.when((r2 != row + 1) & (r2 != row - 1))
        def _():
            greet({"row": r2})
    greet(across)
    near_rows = jnp.where(row > 0, 1, 0) + jnp.where(row < rows - 1, 1, 0)
    near_cols = jnp.where(col > 0, 1, 0) + jnp.where(col < cols - 1, 1, 0)
    pl.semaphore_wait(barrier, 11 + near_cols + near_rows * near_cols)

    lane = lax.broadcasted_iota(jnp.int32, (H, H), 1)
    low = lane < 64
    lane64 = lax.broadcasted_iota(jnp.int32, (64, H), 1)
    low64 = lane64 < 64

    def fold(t, keep_low):
        first, second = t
        n = first.shape[0]
        m = low if n == H else low64
        return jnp.where(m if keep_low else ~m, first, pltpu.roll(second, 64, 1))

    def halo_copy(i, e):
        dr, dc = SIDES[i]
        to = {"row": row + dr, "col": col + dc}
        if dc == 0:
            src, dst = obj.at[e, :, pl.ds(0 if dr < 0 else N - HALO, HALO), :], halo_rows.at[i, e]
        elif dr == 0:
            src, dst = cols_out.at[i - 2, e], halo_cols.at[i - 2, e]
        else:
            src, dst = corners_out.at[i - 4, e], halo_corners.at[i - 4, e]
        return pltpu.make_async_remote_copy(
            src_ref=src, dst_ref=dst, send_sem=halo_send.at[i, e], recv_sem=halo_recv.at[i, e],
            device_id=to, device_id_type=MESH,
        )

    for e in range(4):
        loads[e].wait()
        for i, dc in ((2, -1), (3, 1)):
            at = pl.ds(0 if dc < 0 else H, H)
            for c in (0, 1):
                cols_out[i - 2, e, c] = fold((obj[e, c, :H, at], obj[e, c, H:, at]), dc < 0)
        for i in range(4, 8):
            dr, dc = SIDES[i]
            at = pl.ds(0 if dc < 0 else H, H)
            rr = pl.ds(0 if dr < 0 else N - HALO, HALO)
            corners_out[i - 4, e] = fold((obj[e, 0, rr, at], obj[e, 1, rr, at]), dc < 0)
        for i, (dr, dc) in enumerate(SIDES):
            @pl.when(inside(dr, dc))
            def _():
                halo_copy(i, e).start()

    expand_kernel(kk, kx)
    opad[:, :, :32, :] = jnp.zeros((2, 3, 32, H), F32)
    opad[:, :, 288:, :] = jnp.zeros((2, 3, 32, H), F32)
    loads[4].wait()
    loads[5].wait()
    loads[6].wait()
    pg[...] = jnp.zeros_like(pg)

    def assemble(e):
        pltpu.make_async_copy(amp_any.at[e, 0, 0], amp.at[e], load_sem.at[7 + e]).wait()
        grad[...] = jnp.zeros_like(grad)
        for c in (0, 1):
            for j in (0, 1):
                ext[c, 1 + j, pl.ds(64, N), :] = obj[e, c, :, pl.ds(j * H, H)]
        for i, (dr, dc) in enumerate(SIDES):
            rr = pl.ds(64, N) if dr == 0 else pl.ds(0 if dr > 0 else 320, 64)
            tile = 0 if dc > 0 else 3

            @pl.when(inside(-dr, -dc))
            def _():
                halo_copy(i, e).wait_recv()
                for c in (0, 1):
                    if dc == 0:
                        for j in (0, 1):
                            ext[c, 1 + j, rr, :] = halo_rows[i, e, c, :, pl.ds(j * H, H)]
                    elif dr == 0:
                        v = halo_cols[i - 2, e, c]
                        ext[c, tile, pl.ds(64, H), :] = v
                        ext[c, tile, pl.ds(64 + H, H), :] = pltpu.roll(v, 64, 1)
                    else:
                        v = halo_corners[i - 4, e]
                        ext[c, tile, rr, :] = v if c == 0 else pltpu.roll(v, 64, 1)

            @pl.when(jnp.logical_not(inside(-dr, -dc)))
            def _():
                for c in (0, 1):
                    for t in ((1, 2) if dc == 0 else (tile,)):
                        ext[c, t, rr, :] = jnp.zeros((256 if dr == 0 else 64, H), F32)

    def grad_copy(i, e):
        dr, dc = SIDES[i]
        to = {"row": row + dr, "col": col + dc}
        if dc == 0:
            src, dst = gr_out.at[i, e], gr_in.at[i, e]
        elif dr == 0:
            src, dst = gc_out.at[i - 2, e], gc_in.at[i - 2, e]
        else:
            src, dst = gk_out.at[i - 4, e], gk_in.at[i - 4, e]
        return pltpu.make_async_remote_copy(
            src_ref=src, dst_ref=dst, send_sem=grad_send.at[i, e], recv_sem=grad_recv.at[i, e],
            device_id=to, device_id_type=MESH,
        )

    def hand_over(e):
        for i, (dr, dc) in enumerate(SIDES):
            rr = pl.ds(0 if dr < 0 else 320, 64)
            tile = 0 if dc < 0 else 3

            @pl.when(inside(dr, dc))
            def _():
                if dc == 0:
                    for c in (0, 1):
                        for j in (0, 1):
                            gr_out[i, e, c, :, pl.ds(j * H, H)] = grad[c, 1 + j, rr, :]
                elif dr == 0:
                    for c in (0, 1):
                        gc_out[i - 2, e, c] = fold(
                            (grad[c, tile, pl.ds(64, H), :], grad[c, tile, pl.ds(64 + H, H), :]), dc > 0
                        )
                else:
                    gk_out[i - 4, e] = fold((grad[0, tile, rr, :], grad[1, tile, rr, :]), dc > 0)
                grad_copy(i, e).start()
        for c in (0, 1):
            for j in (0, 1):
                at = pl.ds(j * H, H)
                stepped[e, c, :, at] = obj[e, c, :, at] - STEP * grad[c, 1 + j, pl.ds(64, N), :]

    def in_copy(slot, e):
        to, _ = peer(slot)
        return pltpu.make_async_remote_copy(
            src_ref=stepped.at[e, :, pl.ds(pl.multiple_of(32 * to, 32), 32), :],
            dst_ref=gathered.at[e, me],
            send_sem=in_send.at[slot - 1, e], recv_sem=in_recv.at[slot - 1, e],
            device_id={"energy": to}, device_id_type=MESH,
        )

    def finish(e):
        for i, (dr, dc) in enumerate(SIDES):
            rr = pl.ds(0 if dr > 0 else N - HALO, HALO)
            at = pl.ds(0 if dc > 0 else H, H)

            @pl.when(inside(-dr, -dc))
            def _():
                grad_copy(i, e).wait_recv()
                for c in (0, 1):
                    if dc == 0:
                        stepped[e, c, rr, :] -= STEP * gr_in[i, e, c]
                    elif dr == 0:
                        v = gc_in[i - 2, e, c]
                        m = low if dc > 0 else ~low
                        stepped[e, c, pl.ds(0, H), at] -= STEP * jnp.where(m, v, 0.0)
                        stepped[e, c, pl.ds(H, H), at] -= STEP * jnp.where(m, pltpu.roll(v, 64, 1), 0.0)
                    else:
                        v = gk_in[i - 4, e]
                        v = v if c == 0 else pltpu.roll(v, 64, 1)
                        stepped[e, c, rr, at] -= STEP * jnp.where(low64 if dc > 0 else ~low64, v, 0.0)
        for slot in (4, 5, 2, 6, 3, 7, 1):
            in_copy(slot, e).start()
        gathered[e, me] = stepped[e, :, pl.ds(pl.multiple_of(32 * me, 32), 32), :]

    mine = 128 * core

    def p_copy(step, batch, i):
        es = pl.ds(2 * batch, 2)
        index = (0, 1, 4, 5, 8)[step] + (i - 1 if i else 0)
        if step == 0:
            theirs = pl.ds(pl.multiple_of(128 * (1 - core), 128), 128)
            src, dst, to = pg.at[es, :, theirs, :], core_in.at[batch], partner
        elif step == 1:
            r2 = lax.rem(row + i, rows)
            src = pg.at[es, :, pl.ds(pl.multiple_of(mine + 32 * r2, 32), 32), :]
            dst, to = row_in.at[batch, i - 1], {"row": r2}
        elif step == 2:
            src = pg.at[es, :, pl.ds(pl.multiple_of(mine + 32 * row, 32), 32), :]
            dst, to = far_in.at[batch], across
        elif step == 3:
            src = total.at[es, :, pl.ds(pl.multiple_of(mine + 32 * row, 32), 32), :]
            dst, to = src, {"row": lax.rem(row + i, rows)}
        else:
            src = total.at[es, :, pl.ds(pl.multiple_of(mine, 128), 128), :]
            dst, to = src, partner
        return pltpu.make_async_remote_copy(
            src_ref=src, dst_ref=dst, send_sem=p_send.at[batch, index], recv_sem=p_recv.at[batch, index],
            device_id=to, device_id_type=MESH,
        )

    def probe_step(step, batch):
        es = pl.ds(2 * batch, 2)
        chunk = pl.ds(pl.multiple_of(mine + 32 * row, 32), 32)
        if step == 0:
            p_copy(0, batch, 0).start()
        elif step == 1:
            p_copy(0, batch, 0).wait_recv()
            half = pl.ds(pl.multiple_of(mine, 128), 128)
            pg[es, :, half, :] += core_in[batch]
            for i in (2, 1, 3):
                p_copy(1, batch, i).start()
        elif step == 2:
            for i in (1, 2, 3):
                p_copy(1, batch, i).wait_recv()
            pg[es, :, chunk, :] += row_in[batch, 0] + row_in[batch, 1] + row_in[batch, 2]
            p_copy(2, batch, 0).start()
        elif step == 3:
            p_copy(2, batch, 0).wait_recv()
            total[es, :, chunk, :] = pg[es, :, chunk, :] + far_in[batch]
            for i in (2, 1, 3):
                p_copy(3, batch, i).start()
        else:
            for i in (1, 2, 3):
                p_copy(3, batch, i).wait_recv()
            p_copy(4, batch, 0).start()

    def body(t, _):
        e, k = lax.div(t, 4), lax.rem(t, 4)

        @pl.when(k == 0)
        def _():
            assemble(e)

        position(
            k, offs[0, 0, k, 0], offs[0, 0, k, 1], ext, probe.at[:, e], amp.at[e, k], grad, pg.at[e],
            tab, order, win, exi, ra, rb, la, lb, ap, asc, opad,
        )

        @pl.when(k == 3)
        def _():
            hand_over(e)

        @pl.when((k == 1) & (e > 0))
        def _():
            finish(e - 1)

        for step, when in enumerate((7, 9, 11, 13)):
            @pl.when(t == when)
            def _():
                probe_step(step, 0)
        return 0

    lax.fori_loop(0, 16, body, 0)
    probe_step(0, 1)
    probe_step(4, 0)
    probe_step(1, 1)
    finish(3)

    def half_product(g, half):
        x = gathered[pl.ds(2 * half, 2), :, :, pl.ds(8 * g, 8), :].reshape(N, N)
        hi, lo = split(x)
        k_hi, k_lo = kx[0, :, pl.ds(N * half, N)], kx[1, :, pl.ds(N * half, N)]
        return dot(
            jnp.concatenate([k_hi, k_lo, k_hi], axis=1), jnp.concatenate([hi, hi, lo], axis=0)
        )

    for e in (0, 1):
        for slot in range(1, 8):
            in_copy(slot, e).wait_recv()
    for g in range(4):
        acc[g] = half_product(g, 0)
    probe_step(2, 1)
    for e in (2, 3):
        for slot in range(1, 8):
            in_copy(slot, e).wait_recv()

    def out_copy(slot, g):
        to, _ = peer(slot)
        return pltpu.make_async_remote_copy(
            src_ref=coupled.at[to, :, :, pl.ds(8 * g, 8), :],
            dst_ref=returned.at[:, :, pl.ds(pl.multiple_of(32 * me + 8 * g, 8), 8), :],
            send_sem=out_send.at[slot - 1, g], recv_sem=out_recv.at[slot - 1, g],
            device_id={"energy": to}, device_id_type=MESH,
        )

    for g in range(4):
        out = acc[g] + half_product(g, 1)
        coupled[:, :, :, pl.ds(8 * g, 8), :] = out.reshape(8, 2, 4, 8, N)
        for slot in (4, 5, 2, 6, 3, 7, 1):
            out_copy(slot, g).start()
    own = pl.ds(pl.multiple_of(32 * me, 32), 32)
    returned[:, :, own, :] = coupled[me]
    probe_step(3, 1)
    probe_step(4, 1)
    rate = PROBE_STEP / (4 * rows * cols)
    for batch in (0, 1):
        p_copy(4, batch, 0).wait_recv()
    for e in range(4):
        for c in (0, 1):
            probe[c, e] -= rate * total[e, c]
    stores = [pltpu.make_async_copy(probe, new_probe_any, store_sem.at[0])]
    for copy in stores:
        copy.start()
    for batch in (0, 1):
        for step in range(5):
            for i in ((0,) if step in (0, 2, 4) else (1, 2, 3)):
                p_copy(step, batch, i).wait_send()
    for i, (dr, dc) in enumerate(SIDES):
        @pl.when(inside(dr, dc))
        def _():
            for e in range(4):
                halo_copy(i, e).wait_send()
                grad_copy(i, e).wait_send()
    for e in range(4):
        for slot in range(1, 8):
            in_copy(slot, e).wait_send()
    for g in range(4):
        for slot in range(1, 8):
            out_copy(slot, g).wait_recv()
    for c in (0, 1):
        for e in range(4):
            returned[c, e] += stepped[e, c]
    final = pltpu.make_async_copy(returned, blended_any, store_sem.at[1])
    final.start()
    for g in range(4):
        for slot in range(1, 8):
            out_copy(slot, g).wait_send()
    for copy in stores:
        copy.wait()
    final.wait()


def local(object_field, probe_field, amplitudes, kk_kernel, offsets):
    tab, order = tables()
    vm = lambda *shape: pltpu.VMEM(shape, F32)
    vb = lambda *shape: pltpu.VMEM(shape, BF)
    dma = pltpu.SemaphoreType.DMA
    anywhere = pl.BlockSpec(memory_space=pl.ANY)
    return pl.pallas_call(
        kernel,
        in_specs=[
            pl.BlockSpec(memory_space=pltpu.SMEM), anywhere, anywhere, anywhere,
            pl.BlockSpec(memory_space=pltpu.VMEM), anywhere, anywhere,
        ],
        out_specs=[anywhere, anywhere],
        out_shape=[
            jax.ShapeDtypeStruct(object_field.shape, F32),
            jax.ShapeDtypeStruct(probe_field.shape, F32),
        ],
        scratch_shapes=[
            vm(4, 2, N, N), vm(2, 4, N, N), vm(4, 4, N, N), vb(2, 2, 2, N, N), vb(N, N), vb(2, 512, 512),
            vm(2, 4, 2, 64, N), vm(2, 4, 2, H, H), vm(4, 4, 64, H), vm(2, 4, 2, H, H), vm(4, 4, 64, H),
            vm(2, 4, 2, 64, N), vm(2, 4, 2, H, H), vm(4, 4, 64, H),
            vm(2, 4, 2, 64, N), vm(2, 4, 2, H, H), vm(4, 4, 64, H),
            vm(2, 4, 384, H), vm(2, 4, 384, H), vm(4, 2, N, N), vm(4, 8, 2, 32, N), vm(4, 512, N),
            vm(8, 2, 4, 32, N), vm(2, 4, N, N),
            vm(4, 2, N, N), vm(2, 2, 2, H, N), vm(2, 3, 2, 2, 32, N), vm(2, 2, 2, 32, N), vm(4, 2, N, N),
            vm(2, N, N), vm(2, N, N), vb(N, 2 * N), vb(N, 2 * N), vb(2 * N, N), vb(2 * N, N),
            vb(N, 2 * N), vm(2, N, H), vm(2, 3, 320, H),
            dma((11,)), dma((8, 4)), dma((8, 4)), dma((8, 4)), dma((8, 4)),
            dma((7, 4)), dma((7, 4)), dma((7, 4)), dma((7, 4)),
            dma((2, 9)), dma((2, 9)), dma((2,)),
        ],
        compiler_params=pltpu.CompilerParams(
            collective_id=0, has_side_effects=True, vmem_limit_bytes=64 * 2**20 - 128 * 1024
        ),
        name="gradient_step",
    )(
        offsets, object_field, probe_field, amplitudes, kk_kernel,
        jnp.asarray(tab), jnp.asarray(order),
    )


def solution(mesh):
    return jax.shard_map(
        local,
        mesh=mesh,
        in_specs=(
            P(None, "energy", "row", "col"),
            P(None, "energy", None, None),
            P("energy", "row", "col", None, None, None),
            P(),
            P("row", "col", None, None),
        ),
        out_specs=(P(None, "energy", "row", "col"), P(None, "energy", None, None)),
        check_vma=False,
    )
```

```python
import functools

import jax
import jax.numpy as jnp
import numpy as np
from jax import lax
from jax.experimental import pallas as pl
from jax.experimental.pallas import tpu as pltpu
from jax.sharding import PartitionSpec as P

H = 128
N = 256
HALO = 64
STEP = 0.25
PROBE_STEP = 0.5
FLOOR = 0.25
F32 = jnp.float32
BF = jnp.bfloat16
MESH = pl.DeviceIdType.MESH
SIDES = ((-1, 0), (1, 0), (0, -1), (0, 1), (-1, -1), (-1, 1), (1, -1), (1, 1))


def tables():
    n = np.arange(H)[:, None].astype(np.float64)
    k = np.arange(H)[None, :].astype(np.float64)
    out = []
    for odd in (0, 1):
        angle = -2.0 * np.pi * ((n * (2 * k + odd)) % N) / N
        re, im = np.cos(angle) / 16.0, np.sin(angle) / 16.0
        out.append(np.block([[re, im], [-im, re]]))
    right = np.stack(out)
    both = np.stack([right, np.swapaxes(right, 1, 2)])
    hi = both.astype(np.float32).astype(jnp.bfloat16)
    lo = (both - hi.astype(np.float64)).astype(np.float32).astype(jnp.bfloat16)
    order = np.zeros((N, N), np.float32)
    for lane in range(H):
        order[2 * lane, lane] = 1
        order[2 * lane + 1, H + lane] = 1
    return np.stack([hi, lo], axis=2), order.astype(jnp.bfloat16)


def split(x):
    hi = x.astype(BF)
    return hi, (x - hi.astype(F32)).astype(BF)


def dot(a, b):
    return jnp.dot(a, b, preferred_element_type=F32)


def times_table(q, tab, side, odd):
    hi, lo = tab[side, odd, 0], tab[side, odd, 1]
    return dot(
        jnp.concatenate([q[...], q[:, :N]], axis=1), jnp.concatenate([hi, hi, lo], axis=0)
    )


def table_times(tab, side, odd, q):
    hi, lo = tab[side, odd, 0], tab[side, odd, 1]
    return dot(
        jnp.concatenate([hi, hi, lo], axis=1), jnp.concatenate([q[...], q[:N, :]], axis=0)
    )


def forward(k, a, b, ext, probe, amp, tab, order, win, exi, ra, rb, la, lb, ap, asc, opad):
    base = lax.rem(k, 2)
    s = b + HALO - H * base
    rows_at = 64
    lane = lax.broadcasted_iota(jnp.int32, (rows_at, H), 1)
    keep = lane < H - s
    for rc in range(0, N, rows_at):
        rows = pl.ds(rc, rows_at)
        w = []
        for c in (0, 1):
            t = [pltpu.roll(ext[c, base + j, pl.ds(a + rc, rows_at), :], H - s, 1) for j in range(3)]
            w.append([jnp.where(keep, t[j], t[j + 1]) for j in (0, 1)])
        x = [[None, None], [None, None]]
        for j in (0, 1):
            cols = pl.ds(j * H, H)
            pr, pi = probe[0, rows, cols], probe[1, rows, cols]
            wr, wi = w[0][j], w[1][j]
            win[0, rows, cols] = wr
            win[1, rows, cols] = wi
            x[0][j] = pr * wr - pi * wi
            x[1][j] = pr * wi + pi * wr
            exi[0, rows, cols] = x[0][j]
            exi[1, rows, cols] = x[1][j]
        for c in (0, 1):
            for q, v in ((ra, x[c][0] + x[c][1]), (rb, x[c][0] - x[c][1])):
                hi, lo = split(v)
                q[rows, pl.ds(c * H, H)] = hi
                q[rows, pl.ds(N + c * H, H)] = lo
        hi, lo = split(amp[rows, :])
        ap[rows, pl.ds(0, N)] = hi
        ap[rows, pl.ds(N, N)] = lo
    yield
    y = [times_table(ra, tab, 0, 0), times_table(rb, tab, 0, 1)]
    amps = dot(ap[...], jnp.concatenate([order[...], order[...]], axis=0))
    yield
    for pc in (0, 1):
        cols = pl.ds(pc * H, H)
        for c in (0, 1):
            t = y[pc][:H, c * H:(c + 1) * H]
            u = y[pc][H:, c * H:(c + 1) * H]
            for q, v in ((la, t + u), (lb, t - u)):
                hi, lo = split(v)
                q[pl.ds(c * H, H), cols] = hi
                q[pl.ds(N + c * H, H), cols] = lo
    asc[0] = amps[:, :H]
    asc[1] = amps[:, H:]
    yield
    z = [table_times(tab, 1, 0, la), table_times(tab, 1, 1, lb)]
    yield
    for pr, q in ((0, la), (1, lb)):
        fr, fi = z[pr][:H], z[pr][H:]
        measured = jnp.concatenate([asc[j, pl.ds(pr, H, stride=2), :] for j in (0, 1)], axis=1)
        scale = measured * lax.rsqrt(jnp.maximum(fr * fr + fi * fi, FLOOR * FLOOR))
        for c, v in ((0, fr * scale), (1, fi * scale)):
            hi, lo = split(v)
            q[pl.ds(c * H, H), :] = hi
            q[pl.ds(N + c * H, H), :] = lo
    yield


def backward(k, a, b, probe, grad, pg, tab, win, exi, ra, rb, la, lb, ap, asc, opad):
    base = lax.rem(k, 2)
    s = b + HALO - H * base
    rows_at = 64
    lane = lax.broadcasted_iota(jnp.int32, (rows_at, H), 1)
    p, q = table_times(tab, 0, 0, la), table_times(tab, 0, 1, lb)
    yield
    for half, v in ((0, p + q), (1, p - q)):
        rows = pl.ds(half * H, H)
        for pc, dst in ((0, ra), (1, rb)):
            for c in (0, 1):
                hi, lo = split(v[c * H:(c + 1) * H, pc * H:(pc + 1) * H])
                dst[rows, pl.ds(c * H, H)] = hi
                dst[rows, pl.ds(N + c * H, H)] = lo
    yield
    p, q = times_table(ra, tab, 1, 0), times_table(rb, tab, 1, 1)
    yield
    back = (p + q, p - q)
    turned = lane >= s
    for rc in range(0, N, rows_at):
        rows = pl.ds(rc, rows_at)
        step = [[None] * 2, [None] * 2]
        for j in (0, 1):
            cols = pl.ds(j * H, H)
            dr = exi[0, rows, cols] - back[j][rc:rc + rows_at, :H]
            di = exi[1, rows, cols] - back[j][rc:rc + rows_at, H:]
            pr, pi = probe[0, rows, cols], probe[1, rows, cols]
            wr, wi = win[0, rows, cols], win[1, rows, cols]
            pg[0, rows, cols] += wr * dr + wi * di
            pg[1, rows, cols] += wr * di - wi * dr
            step[0][j] = pltpu.roll(pr * dr + pi * di, s, 1)
            step[1][j] = pltpu.roll(pr * di - pi * dr, s, 1)
        for c in (0, 1):
            at = pl.ds(32 + rc, rows_at)
            opad[c, 0, at, :] = jnp.where(turned, step[c][0], 0.0)
            opad[c, 1, at, :] = jnp.where(turned, step[c][1], step[c][0])
            opad[c, 2, at, :] = jnp.where(turned, 0.0, step[c][1])
    yield
    first = 96 * lax.div(k, 2)
    start = 32 - jnp.clip(a - first, 0, 32)
    for c in (0, 1):
        for j in range(3):
            for rc in range(0, 288, 32):
                at = pl.ds(pl.multiple_of(first + rc, 32), 32)
                grad[c, base + j, at, :] += opad[c, j, pl.ds(start + rc, 32), :]
    yield


ORDER = "frfrrffrrf"


def together(order, back, forth=None):
    for which in order:
        if which == "r":
            next(back)
        elif forth is not None:
            next(forth)


def expand_kernel(kk, kx):
    out_row = lax.broadcasted_iota(jnp.int32, (512, 32), 0)
    out_col = lax.broadcasted_iota(jnp.int32, (512, 32), 1)
    out_energy = 4 * (out_row >> 6) + ((out_row >> 3) & 3)
    in_row = lax.broadcasted_iota(jnp.int32, (32, 512), 0)
    in_col = lax.broadcasted_iota(jnp.int32, (32, 512), 1)
    in_energy = 4 * ((in_col >> 4) & 7) + (in_col >> 7)
    r = lax.broadcasted_iota(jnp.int32, (512, 512), 0)
    c = lax.broadcasted_iota(jnp.int32, (512, 512), 1)
    same = (r & 7) == (c & 7)
    one = lambda m: jnp.where(m, 1.0, 0.0).astype(BF)
    pick = [one((in_energy == in_row) & (((in_col >> 3) & 1) == b)) for b in (0, 1)]
    place = [one((out_energy == out_col) & (((out_row >> 5) & 1) == a)) for a in (0, 1)]
    parts = [[split(kk[a, b]) for b in (0, 1)] for a in (0, 1)]
    for which in (0, 1):
        total = None
        for a in (0, 1):
            row = dot(parts[a][0][which], pick[0]) + dot(parts[a][1][which], pick[1])
            term = dot(place[a], row.astype(BF))
            total = term if total is None else total + term
        kx[which] = jnp.where(same, total, 0.0).astype(BF)


def kernel(
    offs, obj_any, probe_any, amp_any, kk, tab_any, order_any,
    blended, new_probe,
    obj, probe, amp, tab, order, kx,
    halo_rows, halo_cols, halo_corners, cols_out, corners_out,
    gr_in, gc_in, gk_in, gr_out, gc_out, gk_out,
    ext, grad, stepped, gathered, acc, coupled, returned,
    pg, core_in, row_in, far_in, total,
    load_sem, halo_send, halo_recv, grad_send, grad_recv,
    in_send, in_recv, out_send, out_recv, p_send, p_recv,
    *work,
):
    work_a, work_b = work[:9], work[9:]
    me = lax.axis_index("energy")
    row = lax.axis_index("row")
    col = lax.axis_index("col")
    rows, cols = lax.axis_size("row"), lax.axis_size("col")
    core = lax.rem(col, 2)
    partner = {"col": col + 1 - 2 * core}
    high = lax.div(col, 2)
    across = {"col": col + 2 - 4 * high}

    def peer(slot):
        dx, dy = slot // 2, slot % 2
        x, y = lax.div(me, 2), lax.rem(me, 2)
        y2 = y + dy * (1 - 2 * y)
        return lax.rem(x + dx, 4) * 2 + y2, lax.rem(x + 4 - dx, 4) * 2 + y2

    def inside(dr, dc):
        ok = None
        for d, at, n in ((dr, row, rows), (dc, col, cols)):
            if d:
                here = at > 0 if d < 0 else at < n - 1
                ok = here if ok is None else ok & here
        return ok

    loads = []
    for e in range(4):
        loads.append(pltpu.make_async_copy(obj_any.at[:, e], obj.at[e], load_sem.at[e]))
    loads.append(pltpu.make_async_copy(probe_any, probe, load_sem.at[4]))
    loads.append(pltpu.make_async_copy(tab_any, tab, load_sem.at[5]))
    loads.append(pltpu.make_async_copy(order_any, order, load_sem.at[6]))
    for e in range(4):
        loads.append(pltpu.make_async_copy(amp_any.at[e, 0, 0], amp.at[e], load_sem.at[7 + e]))
    for copy in loads:
        copy.start()

    barrier = pltpu.get_barrier_semaphore()

    def greet(device):
        pl.semaphore_signal(barrier, inc=1, device_id=device, device_id_type=MESH)

    for dr, dc in SIDES:
        @pl.when(inside(dr, dc))
        def _():
            greet({"row": row + dr, "col": col + dc})
    for slot in range(1, 8):
        greet({"energy": peer(slot)[0]})
    for d in range(1, 4):
        r2 = lax.rem(row + d, rows)

        @pl.when((r2 != row + 1) & (r2 != row - 1))
        def _():
            greet({"row": r2})
    greet(across)
    near_rows = jnp.where(row > 0, 1, 0) + jnp.where(row < rows - 1, 1, 0)
    near_cols = jnp.where(col > 0, 1, 0) + jnp.where(col < cols - 1, 1, 0)
    pl.semaphore_wait(barrier, 11 + near_cols + near_rows * near_cols)

    lane = lax.broadcasted_iota(jnp.int32, (H, H), 1)
    low = lane < 64
    lane64 = lax.broadcasted_iota(jnp.int32, (64, H), 1)
    low64 = lane64 < 64

    def fold(t, keep_low):
        first, second = t
        n = first.shape[0]
        m = low if n == H else low64
        return jnp.where(m if keep_low else ~m, first, pltpu.roll(second, 64, 1))

    def halo_copy(i, e):
        dr, dc = SIDES[i]
        to = {"row": row + dr, "col": col + dc}
        if dc == 0:
            src, dst = obj.at[e, :, pl.ds(0 if dr < 0 else N - HALO, HALO), :], halo_rows.at[i, e]
        elif dr == 0:
            src, dst = cols_out.at[i - 2, e], halo_cols.at[i - 2, e]
        else:
            src, dst = corners_out.at[i - 4, e], halo_corners.at[i - 4, e]
        return pltpu.make_async_remote_copy(
            src_ref=src, dst_ref=dst, send_sem=halo_send.at[i, e], recv_sem=halo_recv.at[i, e],
            device_id=to, device_id_type=MESH,
        )

    for e in range(4):
        loads[e].wait()
        for i, dc in ((2, -1), (3, 1)):
            at = pl.ds(0 if dc < 0 else H, H)
            for c in (0, 1):
                cols_out[i - 2, e, c] = fold((obj[e, c, :H, at], obj[e, c, H:, at]), dc < 0)
        for i in range(4, 8):
            dr, dc = SIDES[i]
            at = pl.ds(0 if dc < 0 else H, H)
            rr = pl.ds(0 if dr < 0 else N - HALO, HALO)
            corners_out[i - 4, e] = fold((obj[e, 0, rr, at], obj[e, 1, rr, at]), dc < 0)
        for i, (dr, dc) in enumerate(SIDES):
            @pl.when(inside(dr, dc))
            def _():
                halo_copy(i, e).start()

    expand_kernel(kk, kx)
    for buffers in (work_a, work_b):
        opad = buffers[8]
        opad[:, :, :32, :] = jnp.zeros((2, 3, 32, H), F32)
        opad[:, :, 288:, :] = jnp.zeros((2, 3, 32, H), F32)
    for part in (0, 1, 4, 5):
        work_b[part][...] = jnp.zeros_like(work_b[part])
    grad[...] = jnp.zeros_like(grad)
    loads[4].wait()
    loads[5].wait()
    loads[6].wait()
    pg[...] = jnp.zeros_like(pg)

    def assemble(e):
        pltpu.make_async_copy(amp_any.at[e, 0, 0], amp.at[e], load_sem.at[7 + e]).wait()
        for c in (0, 1):
            for j in (0, 1):
                ext[c, 1 + j, pl.ds(64, N), :] = obj[e, c, :, pl.ds(j * H, H)]
        for i, (dr, dc) in enumerate(SIDES):
            rr = pl.ds(64, N) if dr == 0 else pl.ds(0 if dr > 0 else 320, 64)
            tile = 0 if dc > 0 else 3

            @pl.when(inside(-dr, -dc))
            def _():
                halo_copy(i, e).wait_recv()
                for c in (0, 1):
                    if dc == 0:
                        for j in (0, 1):
                            ext[c, 1 + j, rr, :] = halo_rows[i, e, c, :, pl.ds(j * H, H)]
                    elif dr == 0:
                        v = halo_cols[i - 2, e, c]
                        ext[c, tile, pl.ds(64, H), :] = v
                        ext[c, tile, pl.ds(64 + H, H), :] = pltpu.roll(v, 64, 1)
                    else:
                        v = halo_corners[i - 4, e]
                        ext[c, tile, rr, :] = v if c == 0 else pltpu.roll(v, 64, 1)

            @pl.when(jnp.logical_not(inside(-dr, -dc)))
            def _():
                for c in (0, 1):
                    for t in ((1, 2) if dc == 0 else (tile,)):
                        ext[c, t, rr, :] = jnp.zeros((256 if dr == 0 else 64, H), F32)

    def grad_copy(i, e):
        dr, dc = SIDES[i]
        to = {"row": row + dr, "col": col + dc}
        if dc == 0:
            src, dst = gr_out.at[i, e], gr_in.at[i, e]
        elif dr == 0:
            src, dst = gc_out.at[i - 2, e], gc_in.at[i - 2, e]
        else:
            src, dst = gk_out.at[i - 4, e], gk_in.at[i - 4, e]
        return pltpu.make_async_remote_copy(
            src_ref=src, dst_ref=dst, send_sem=grad_send.at[i, e], recv_sem=grad_recv.at[i, e],
            device_id=to, device_id_type=MESH,
        )

    def hand_over(e):
        for i, (dr, dc) in enumerate(SIDES):
            rr = pl.ds(0 if dr < 0 else 320, 64)
            tile = 0 if dc < 0 else 3

            @pl.when(inside(dr, dc))
            def _():
                if dc == 0:
                    for c in (0, 1):
                        for j in (0, 1):
                            gr_out[i, e, c, :, pl.ds(j * H, H)] = grad[c, 1 + j, rr, :]
                elif dr == 0:
                    for c in (0, 1):
                        gc_out[i - 2, e, c] = fold(
                            (grad[c, tile, pl.ds(64, H), :], grad[c, tile, pl.ds(64 + H, H), :]), dc > 0
                        )
                else:
                    gk_out[i - 4, e] = fold((grad[0, tile, rr, :], grad[1, tile, rr, :]), dc > 0)
                grad_copy(i, e).start()
        for c in (0, 1):
            for j in (0, 1):
                at = pl.ds(j * H, H)
                stepped[e, c, :, at] = obj[e, c, :, at] - STEP * grad[c, 1 + j, pl.ds(64, N), :]

    def in_copy(slot, e):
        to, _ = peer(slot)
        return pltpu.make_async_remote_copy(
            src_ref=stepped.at[e, :, pl.ds(pl.multiple_of(32 * to, 32), 32), :],
            dst_ref=gathered.at[e, me],
            send_sem=in_send.at[slot - 1, e], recv_sem=in_recv.at[slot - 1, e],
            device_id={"energy": to}, device_id_type=MESH,
        )

    def finish(e):
        for i, (dr, dc) in enumerate(SIDES):
            rr = pl.ds(0 if dr > 0 else N - HALO, HALO)
            at = pl.ds(0 if dc > 0 else H, H)

            @pl.when(inside(-dr, -dc))
            def _():
                grad_copy(i, e).wait_recv()
                for c in (0, 1):
                    if dc == 0:
                        stepped[e, c, rr, :] -= STEP * gr_in[i, e, c]
                    elif dr == 0:
                        v = gc_in[i - 2, e, c]
                        m = low if dc > 0 else ~low
                        stepped[e, c, pl.ds(0, H), at] -= STEP * jnp.where(m, v, 0.0)
                        stepped[e, c, pl.ds(H, H), at] -= STEP * jnp.where(m, pltpu.roll(v, 64, 1), 0.0)
                    else:
                        v = gk_in[i - 4, e]
                        v = v if c == 0 else pltpu.roll(v, 64, 1)
                        stepped[e, c, rr, at] -= STEP * jnp.where(low64 if dc > 0 else ~low64, v, 0.0)
        for slot in (4, 5, 2, 6, 3, 7, 1):
            in_copy(slot, e).start()
        gathered[e, me] = stepped[e, :, pl.ds(pl.multiple_of(32 * me, 32), 32), :]

    mine = 128 * core

    def p_copy(step, e, i):
        index = (0, 1, 4, 5, 8)[step] + (i - 1 if i else 0)
        if step == 0:
            theirs = pl.ds(pl.multiple_of(128 * (1 - core), 128), 128)
            src, dst, to = pg.at[e, :, theirs, :], core_in.at[e], partner
        elif step == 1:
            r2 = lax.rem(row + i, rows)
            src = pg.at[e, :, pl.ds(pl.multiple_of(mine + 32 * r2, 32), 32), :]
            dst, to = row_in.at[e, i - 1], {"row": r2}
        elif step == 2:
            src = pg.at[e, :, pl.ds(pl.multiple_of(mine + 32 * row, 32), 32), :]
            dst, to = far_in.at[e], across
        elif step == 3:
            src = total.at[e, :, pl.ds(pl.multiple_of(mine + 32 * row, 32), 32), :]
            dst, to = src, {"row": lax.rem(row + i, rows)}
        else:
            src = total.at[e, :, pl.ds(pl.multiple_of(mine, 128), 128), :]
            dst, to = src, partner
        return pltpu.make_async_remote_copy(
            src_ref=src, dst_ref=dst, send_sem=p_send.at[e, index], recv_sem=p_recv.at[e, index],
            device_id=to, device_id_type=MESH,
        )

    def probe_step(step, e):
        chunk = pl.ds(pl.multiple_of(mine + 32 * row, 32), 32)
        if step == 0:
            p_copy(0, e, 0).start()
        elif step == 1:
            p_copy(0, e, 0).wait_recv()
            half = pl.ds(pl.multiple_of(mine, 128), 128)
            pg[e, :, half, :] += core_in[e]
            for i in (2, 1, 3):
                p_copy(1, e, i).start()
        elif step == 2:
            for i in (1, 2, 3):
                p_copy(1, e, i).wait_recv()
            pg[e, :, chunk, :] += row_in[e, 0] + row_in[e, 1] + row_in[e, 2]
            p_copy(2, e, 0).start()
        elif step == 3:
            p_copy(2, e, 0).wait_recv()
            total[e, :, chunk, :] = pg[e, :, chunk, :] + far_in[e]
            for i in (2, 1, 3):
                p_copy(3, e, i).start()
        else:
            for i in (1, 2, 3):
                p_copy(3, e, i).wait_recv()
            p_copy(4, e, 0).start()

    def front(k, e, buffers):
        return forward(
            k, offs[0, 0, 0, k], offs[0, 0, 1, k], ext, probe.at[:, e], amp.at[e, k], tab, order, *buffers
        )

    def rear(k, e, buffers):
        return backward(
            k, offs[0, 0, 0, k], offs[0, 0, 1, k], probe.at[:, e], grad, pg.at[e], tab, *buffers
        )

    def body(t, _):
        e, odd = lax.div(t, 2), lax.rem(t, 2)

        @pl.when(odd == 0)
        def _():
            assemble(e)

        last = jnp.maximum(lax.div(2 * t - 1, 4), 0)
        together(ORDER, rear(3 - 2 * odd, last, work_b), front(2 * odd, e, work_a))

        @pl.when((odd == 0) & (e > 0))
        def _():
            hand_over(e - 1)
            grad[...] = jnp.zeros_like(grad)

        @pl.when((odd == 0) & (e > 1))
        def _():
            finish(e - 2)

        for step in range(3):
            @pl.when((odd == 0) & (e > step))
            def _():
                probe_step(step, e - 1 - step)

        together(ORDER, rear(2 * odd, e, work_a), front(2 * odd + 1, e, work_b))
        return 0

    lax.fori_loop(0, 8, body, 0)
    together(ORDER, rear(3, 3, work_b))
    hand_over(3)
    finish(2)
    for step in range(3):
        probe_step(step, 3 - step)
    finish(3)
    for step in (1, 2):
        probe_step(step, 4 - step)

    def half_product(g, half):
        x = gathered[pl.ds(2 * half, 2), :, :, pl.ds(8 * g, 8), :].reshape(N, N)
        hi, lo = split(x)
        k_hi, k_lo = kx[0, :, pl.ds(N * half, N)], kx[1, :, pl.ds(N * half, N)]
        return dot(
            jnp.concatenate([k_hi, k_lo, k_hi], axis=1), jnp.concatenate([hi, hi, lo], axis=0)
        )

    for e in (0, 1):
        for slot in range(1, 8):
            in_copy(slot, e).wait_recv()
    for g in range(4):
        acc[g] = half_product(g, 0)
    for e in (2, 3):
        for slot in range(1, 8):
            in_copy(slot, e).wait_recv()

    probe_step(2, 3)

    def out_copy(slot, g):
        to, _ = peer(slot)
        return pltpu.make_async_remote_copy(
            src_ref=coupled.at[to, :, :, pl.ds(8 * g, 8), :],
            dst_ref=returned.at[:, :, me, pl.ds(8 * g, 8), :],
            send_sem=out_send.at[slot - 1, g], recv_sem=out_recv.at[slot - 1, g],
            device_id={"energy": to}, device_id_type=MESH,
        )

    for g in range(4):
        out = acc[g] + half_product(g, 1)
        coupled[:, :, :, pl.ds(8 * g, 8), :] = out.reshape(8, 2, 4, 8, N)
        for slot in (4, 5, 2, 6, 3, 7, 1):
            out_copy(slot, g).start()
    returned[:, :, me] = coupled[me]
    for step in (3, 4):
        for e in range(4):
            probe_step(step, e)
    rate = PROBE_STEP / (4 * rows * cols)
    for e in range(4):
        p_copy(4, e, 0).wait_recv()
        for c in (0, 1):
            new_probe[c, e] = probe[c, e] - rate * total[e, c]
    for e in range(4):
        for step in range(5):
            for i in ((0,) if step in (0, 2, 4) else (1, 2, 3)):
                p_copy(step, e, i).wait_send()
        for slot in range(1, 8):
            in_copy(slot, e).wait_send()
    for i, (dr, dc) in enumerate(SIDES):
        @pl.when(inside(dr, dc))
        def _():
            for e in range(4):
                halo_copy(i, e).wait_send()
                grad_copy(i, e).wait_send()
    for g in range(4):
        for slot in range(1, 8):
            out_copy(slot, g).wait_recv()
        for c in (0, 1):
            for e in range(4):
                for d in range(8):
                    at = pl.ds(32 * d + 8 * g, 8)
                    blended[c, e, at, :] = stepped[e, c, at, :] + returned[c, e, d, pl.ds(8 * g, 8), :]
    for g in range(4):
        for slot in range(1, 8):
            out_copy(slot, g).wait_send()


def local(object_field, probe_field, amplitudes, kk_kernel, offsets):
    tab, order = tables()
    vm = lambda *shape: pltpu.VMEM(shape, F32)
    vb = lambda *shape: pltpu.VMEM(shape, BF)
    dma = pltpu.SemaphoreType.DMA
    anywhere = pl.BlockSpec(memory_space=pl.ANY)
    return pl.pallas_call(
        kernel,
        in_specs=[
            pl.BlockSpec(memory_space=pltpu.SMEM), anywhere, anywhere, anywhere,
            pl.BlockSpec(memory_space=pltpu.VMEM), anywhere, anywhere,
        ],
        out_specs=[pl.BlockSpec(memory_space=pltpu.VMEM)] * 2,
        out_shape=[pltpu.VMEM(object_field.shape, F32), pltpu.VMEM(probe_field.shape, F32)],
        scratch_shapes=[
            vm(4, 2, N, N), vm(2, 4, N, N), vm(4, 4, N, N), vb(2, 2, 2, N, N), vb(N, N), vb(2, 512, 512),
            vm(2, 4, 2, 64, N), vm(2, 4, 2, H, H), vm(4, 4, 64, H), vm(2, 4, 2, H, H), vm(4, 4, 64, H),
            vm(2, 4, 2, 64, N), vm(2, 4, 2, H, H), vm(4, 4, 64, H),
            vm(2, 4, 2, 64, N), vm(2, 4, 2, H, H), vm(4, 4, 64, H),
            vm(2, 4, 384, H), vm(2, 4, 384, H), vm(4, 2, N, N), vm(4, 8, 2, 32, N), vm(4, 512, N),
            vm(8, 2, 4, 32, N), vm(2, 4, 8, 32, N),
            vm(4, 2, N, N), vm(4, 2, H, N), vm(4, 3, 2, 32, N), vm(4, 2, 32, N), vm(4, 2, N, N),
            dma((11,)), dma((8, 4)), dma((8, 4)), dma((8, 4)), dma((8, 4)),
            dma((7, 4)), dma((7, 4)), dma((7, 4)), dma((7, 4)), dma((4, 9)), dma((4, 9)),
        ] + 2 * [
            vm(2, N, N), vm(2, N, N), vb(N, 2 * N), vb(N, 2 * N), vb(2 * N, N), vb(2 * N, N),
            vb(N, 2 * N), vm(2, N, H), vm(2, 3, 320, H),
        ],
        compiler_params=pltpu.CompilerParams(
            collective_id=0, has_side_effects=True, vmem_limit_bytes=56 * 2**20
        ),
        name="gradient_step",
    )(
        jnp.swapaxes(offsets, 2, 3), object_field, probe_field, amplitudes, kk_kernel,
        jnp.asarray(tab), jnp.asarray(order),
    )


def solution(mesh):
    return jax.shard_map(
        local,
        mesh=mesh,
        in_specs=(
            P(None, "energy", "row", "col"),
            P(None, "energy", None, None),
            P("energy", "row", "col", None, None, None),
            P(),
            P("row", "col", None, None),
        ),
        out_specs=(P(None, "energy", "row", "col"), P(None, "energy", None, None)),
        check_vma=False,
    )
```

```python
import functools

import jax
import jax.numpy as jnp
import numpy as np
from jax import lax
from jax.experimental import pallas as pl
from jax.experimental.pallas import tpu as pltpu
from jax.sharding import PartitionSpec as P

H = 128
N = 256
HALO = 64
STEP = 0.25
PROBE_STEP = 0.5
FLOOR = 0.25
F32 = jnp.float32
BF = jnp.bfloat16
MESH = pl.DeviceIdType.MESH
SIDES = ((-1, 0), (1, 0), (0, -1), (0, 1), (-1, -1), (-1, 1), (1, -1), (1, 1))


def tables():
    n = np.arange(H)[:, None].astype(np.float64)
    k = np.arange(H)[None, :].astype(np.float64)
    out = []
    for odd in (0, 1):
        angle = -2.0 * np.pi * ((n * (2 * k + odd)) % N) / N
        re, im = np.cos(angle) / 16.0, np.sin(angle) / 16.0
        out.append(np.block([[re, im], [-im, re]]))
    right = np.stack(out)
    both = np.stack([right, np.swapaxes(right, 1, 2)])
    hi = both.astype(np.float32).astype(jnp.bfloat16)
    lo = (both - hi.astype(np.float64)).astype(np.float32).astype(jnp.bfloat16)
    order = np.zeros((N, N), np.float32)
    for lane in range(H):
        order[2 * lane, lane] = 1
        order[2 * lane + 1, H + lane] = 1
    return np.stack([hi, lo], axis=2), order.astype(jnp.bfloat16)


def split(x):
    hi = x.astype(BF)
    return hi, (x - hi.astype(F32)).astype(BF)


def dot(a, b):
    return jnp.dot(a, b, preferred_element_type=F32)


def times_table(q, tab, side, odd):
    hi, lo = tab[side, odd, 0], tab[side, odd, 1]
    return dot(
        jnp.concatenate([q[...], q[:, :N]], axis=1), jnp.concatenate([hi, hi, lo], axis=0)
    )


def table_times(tab, side, odd, q):
    hi, lo = tab[side, odd, 0], tab[side, odd, 1]
    return dot(
        jnp.concatenate([hi, hi, lo], axis=1), jnp.concatenate([q[...], q[:N, :]], axis=0)
    )


def forward(k, a, b, ext, probe, amp, tab, order, win, exi, ra, rb, la, lb, ap, asc, opad):
    base = lax.rem(k, 2)
    s = b + HALO - H * base
    rows_at = 64
    lane = lax.broadcasted_iota(jnp.int32, (rows_at, H), 1)
    keep = lane < H - s
    for rc in range(0, N, rows_at):
        rows = pl.ds(rc, rows_at)
        w = []
        for c in (0, 1):
            t = [pltpu.roll(ext[c, base + j, pl.ds(a + rc, rows_at), :], H - s, 1) for j in range(3)]
            w.append([jnp.where(keep, t[j], t[j + 1]) for j in (0, 1)])
        x = [[None, None], [None, None]]
        for j in (0, 1):
            cols = pl.ds(j * H, H)
            pr, pi = probe[0, rows, cols], probe[1, rows, cols]
            wr, wi = w[0][j], w[1][j]
            win[0, rows, cols] = wr
            win[1, rows, cols] = wi
            x[0][j] = pr * wr - pi * wi
            x[1][j] = pr * wi + pi * wr
            exi[0, rows, cols] = x[0][j]
            exi[1, rows, cols] = x[1][j]
        for c in (0, 1):
            for q, v in ((ra, x[c][0] + x[c][1]), (rb, x[c][0] - x[c][1])):
                hi, lo = split(v)
                q[rows, pl.ds(c * H, H)] = hi
                q[rows, pl.ds(N + c * H, H)] = lo
        hi, lo = split(amp[rows, :])
        ap[rows, pl.ds(0, N)] = hi
        ap[rows, pl.ds(N, N)] = lo
    yield
    y = [times_table(ra, tab, 0, 0), times_table(rb, tab, 0, 1)]
    amps = dot(ap[...], jnp.concatenate([order[...], order[...]], axis=0))
    yield
    for pc in (0, 1):
        cols = pl.ds(pc * H, H)
        for c in (0, 1):
            t = y[pc][:H, c * H:(c + 1) * H]
            u = y[pc][H:, c * H:(c + 1) * H]
            for q, v in ((la, t + u), (lb, t - u)):
                hi, lo = split(v)
                q[pl.ds(c * H, H), cols] = hi
                q[pl.ds(N + c * H, H), cols] = lo
    asc[0] = amps[:, :H]
    asc[1] = amps[:, H:]
    yield
    z = [table_times(tab, 1, 0, la), table_times(tab, 1, 1, lb)]
    yield
    for pr, q in ((0, la), (1, lb)):
        fr, fi = z[pr][:H], z[pr][H:]
        measured = jnp.concatenate([asc[j, pl.ds(pr, H, stride=2), :] for j in (0, 1)], axis=1)
        scale = measured * lax.rsqrt(jnp.maximum(fr * fr + fi * fi, FLOOR * FLOOR))
        for c, v in ((0, fr * scale), (1, fi * scale)):
            hi, lo = split(v)
            q[pl.ds(c * H, H), :] = hi
            q[pl.ds(N + c * H, H), :] = lo
    yield


def backward(k, a, b, probe, grad, pg, tab, win, exi, ra, rb, la, lb, ap, asc, opad):
    base = lax.rem(k, 2)
    s = b + HALO - H * base
    rows_at = 64
    lane = lax.broadcasted_iota(jnp.int32, (rows_at, H), 1)
    p, q = table_times(tab, 0, 0, la), table_times(tab, 0, 1, lb)
    yield
    for half, v in ((0, p + q), (1, p - q)):
        rows = pl.ds(half * H, H)
        for pc, dst in ((0, ra), (1, rb)):
            for c in (0, 1):
                hi, lo = split(v[c * H:(c + 1) * H, pc * H:(pc + 1) * H])
                dst[rows, pl.ds(c * H, H)] = hi
                dst[rows, pl.ds(N + c * H, H)] = lo
    yield
    p, q = times_table(ra, tab, 1, 0), times_table(rb, tab, 1, 1)
    yield
    back = (p + q, p - q)
    turned = lane >= s
    for rc in range(0, N, rows_at):
        rows = pl.ds(rc, rows_at)
        step = [[None] * 2, [None] * 2]
        for j in (0, 1):
            cols = pl.ds(j * H, H)
            dr = exi[0, rows, cols] - back[j][rc:rc + rows_at, :H]
            di = exi[1, rows, cols] - back[j][rc:rc + rows_at, H:]
            pr, pi = probe[0, rows, cols], probe[1, rows, cols]
            wr, wi = win[0, rows, cols], win[1, rows, cols]
            pg[0, rows, cols] += wr * dr + wi * di
            pg[1, rows, cols] += wr * di - wi * dr
            step[0][j] = pltpu.roll(pr * dr + pi * di, s, 1)
            step[1][j] = pltpu.roll(pr * di - pi * dr, s, 1)
        for c in (0, 1):
            at = pl.ds(32 + rc, rows_at)
            opad[c, 0, at, :] = jnp.where(turned, step[c][0], 0.0)
            opad[c, 1, at, :] = jnp.where(turned, step[c][1], step[c][0])
            opad[c, 2, at, :] = jnp.where(turned, 0.0, step[c][1])
    yield
    first = 96 * lax.div(k, 2)
    start = 32 - jnp.clip(a - first, 0, 32)
    for c in (0, 1):
        for j in range(3):
            for rc in range(0, 288, 32):
                at = pl.ds(pl.multiple_of(first + rc, 32), 32)
                grad[c, base + j, at, :] += opad[c, j, pl.ds(start + rc, 32), :]
    yield


ORDER = "frfrrffrrf"


def together(order, back, forth=None):
    for which in order:
        if which == "r":
            next(back)
        elif forth is not None:
            next(forth)


def expand_kernel(kk, kx):
    out_row = lax.broadcasted_iota(jnp.int32, (512, 32), 0)
    out_col = lax.broadcasted_iota(jnp.int32, (512, 32), 1)
    out_energy = 4 * (out_row >> 6) + ((out_row >> 3) & 3)
    in_row = lax.broadcasted_iota(jnp.int32, (32, 512), 0)
    in_col = lax.broadcasted_iota(jnp.int32, (32, 512), 1)
    in_energy = 4 * ((in_col >> 4) & 7) + (in_col >> 7)
    r = lax.broadcasted_iota(jnp.int32, (512, 512), 0)
    c = lax.broadcasted_iota(jnp.int32, (512, 512), 1)
    same = (r & 7) == (c & 7)
    one = lambda m: jnp.where(m, 1.0, 0.0).astype(BF)
    pick = [one((in_energy == in_row) & (((in_col >> 3) & 1) == b)) for b in (0, 1)]
    place = [one((out_energy == out_col) & (((out_row >> 5) & 1) == a)) for a in (0, 1)]
    parts = [[split(kk[a, b]) for b in (0, 1)] for a in (0, 1)]
    for which in (0, 1):
        total = None
        for a in (0, 1):
            row = dot(parts[a][0][which], pick[0]) + dot(parts[a][1][which], pick[1])
            term = dot(place[a], row.astype(BF))
            total = term if total is None else total + term
        kx[which] = jnp.where(same, total, 0.0).astype(BF)


def kernel(
    offs, obj_any, probe_any, amp_any, kk, tab_any, order_any,
    blended, new_probe,
    obj, probe, amp, tab, order, kx,
    halo_rows, halo_cols, halo_corners, cols_out, corners_out,
    gr_in, gc_in, gk_in, gr_out, gc_out, gk_out,
    ext, grad, stepped, gathered, acc, coupled, returned,
    pg, core_in, row_in, far_in, total,
    load_sem, halo_send, halo_recv, grad_send, grad_recv,
    in_send, in_recv, out_send, out_recv, p_send, p_recv,
    *work,
):
    work_a, work_b = work[:9], work[9:]
    me = lax.axis_index("energy")
    row = lax.axis_index("row")
    col = lax.axis_index("col")
    rows, cols = lax.axis_size("row"), lax.axis_size("col")
    core = lax.rem(col, 2)
    partner = {"col": col + 1 - 2 * core}
    high = lax.div(col, 2)
    across = {"col": col + 2 - 4 * high}

    def peer(slot):
        dx, dy = slot // 2, slot % 2
        x, y = lax.div(me, 2), lax.rem(me, 2)
        y2 = y + dy * (1 - 2 * y)
        return lax.rem(x + dx, 4) * 2 + y2, lax.rem(x + 4 - dx, 4) * 2 + y2

    def inside(dr, dc):
        ok = None
        for d, at, n in ((dr, row, rows), (dc, col, cols)):
            if d:
                here = at > 0 if d < 0 else at < n - 1
                ok = here if ok is None else ok & here
        return ok

    loads = []
    for e in range(4):
        loads.append(pltpu.make_async_copy(obj_any.at[:, e], obj.at[e], load_sem.at[e]))
    loads.append(pltpu.make_async_copy(probe_any, probe, load_sem.at[4]))
    loads.append(pltpu.make_async_copy(tab_any, tab, load_sem.at[5]))
    loads.append(pltpu.make_async_copy(order_any, order, load_sem.at[6]))
    for e in range(4):
        loads.append(pltpu.make_async_copy(amp_any.at[e, 0, 0], amp.at[e], load_sem.at[7 + e]))
    for copy in loads:
        copy.start()

    barrier = pltpu.get_barrier_semaphore()

    def greet(device):
        pl.semaphore_signal(barrier, inc=1, device_id=device, device_id_type=MESH)

    for dr, dc in SIDES:
        @pl.when(inside(dr, dc))
        def _():
            greet({"row": row + dr, "col": col + dc})
    for slot in range(1, 8):
        greet({"energy": peer(slot)[0]})
    for d in range(1, 4):
        r2 = lax.rem(row + d, rows)

        @pl.when((r2 != row + 1) & (r2 != row - 1))
        def _():
            greet({"row": r2})
    greet(across)
    near_rows = jnp.where(row > 0, 1, 0) + jnp.where(row < rows - 1, 1, 0)
    near_cols = jnp.where(col > 0, 1, 0) + jnp.where(col < cols - 1, 1, 0)
    pl.semaphore_wait(barrier, 11 + near_cols + near_rows * near_cols)

    lane = lax.broadcasted_iota(jnp.int32, (H, H), 1)
    low = lane < 64
    lane64 = lax.broadcasted_iota(jnp.int32, (64, H), 1)
    low64 = lane64 < 64

    def fold(t, keep_low):
        first, second = t
        n = first.shape[0]
        m = low if n == H else low64
        return jnp.where(m if keep_low else ~m, first, pltpu.roll(second, 64, 1))

    def halo_copy(i, e):
        dr, dc = SIDES[i]
        to = {"row": row + dr, "col": col + dc}
        if dc == 0:
            src, dst = obj.at[e, :, pl.ds(0 if dr < 0 else N - HALO, HALO), :], halo_rows.at[i, e]
        elif dr == 0:
            src, dst = cols_out.at[i - 2, e], halo_cols.at[i - 2, e]
        else:
            src, dst = corners_out.at[i - 4, e], halo_corners.at[i - 4, e]
        return pltpu.make_async_remote_copy(
            src_ref=src, dst_ref=dst, send_sem=halo_send.at[i, e], recv_sem=halo_recv.at[i, e],
            device_id=to, device_id_type=MESH,
        )

    for e in range(4):
        loads[e].wait()
        for i, dc in ((2, -1), (3, 1)):
            at = pl.ds(0 if dc < 0 else H, H)
            for c in (0, 1):
                cols_out[i - 2, e, c] = fold((obj[e, c, :H, at], obj[e, c, H:, at]), dc < 0)
        for i in range(4, 8):
            dr, dc = SIDES[i]
            at = pl.ds(0 if dc < 0 else H, H)
            rr = pl.ds(0 if dr < 0 else N - HALO, HALO)
            corners_out[i - 4, e] = fold((obj[e, 0, rr, at], obj[e, 1, rr, at]), dc < 0)
        for i, (dr, dc) in enumerate(SIDES):
            @pl.when(inside(dr, dc))
            def _():
                halo_copy(i, e).start()

    expand_kernel(kk, kx)
    for buffers in (work_a, work_b):
        opad = buffers[8]
        opad[:, :, :32, :] = jnp.zeros((2, 3, 32, H), F32)
        opad[:, :, 288:, :] = jnp.zeros((2, 3, 32, H), F32)
    for part in (0, 1, 4, 5):
        work_b[part][...] = jnp.zeros_like(work_b[part])
    grad[...] = jnp.zeros_like(grad)
    loads[4].wait()
    loads[5].wait()
    loads[6].wait()
    pg[...] = jnp.zeros_like(pg)

    def assemble(e):
        pltpu.make_async_copy(amp_any.at[e, 0, 0], amp.at[e], load_sem.at[7 + e]).wait()
        for c in (0, 1):
            for j in (0, 1):
                ext[c, 1 + j, pl.ds(64, N), :] = obj[e, c, :, pl.ds(j * H, H)]
        for i, (dr, dc) in enumerate(SIDES):
            rr = pl.ds(64, N) if dr == 0 else pl.ds(0 if dr > 0 else 320, 64)
            tile = 0 if dc > 0 else 3

            @pl.when(inside(-dr, -dc))
            def _():
                halo_copy(i, e).wait_recv()
                for c in (0, 1):
                    if dc == 0:
                        for j in (0, 1):
                            ext[c, 1 + j, rr, :] = halo_rows[i, e, c, :, pl.ds(j * H, H)]
                    elif dr == 0:
                        v = halo_cols[i - 2, e, c]
                        ext[c, tile, pl.ds(64, H), :] = v
                        ext[c, tile, pl.ds(64 + H, H), :] = pltpu.roll(v, 64, 1)
                    else:
                        v = halo_corners[i - 4, e]
                        ext[c, tile, rr, :] = v if c == 0 else pltpu.roll(v, 64, 1)

            @pl.when(jnp.logical_not(inside(-dr, -dc)))
            def _():
                for c in (0, 1):
                    for t in ((1, 2) if dc == 0 else (tile,)):
                        ext[c, t, rr, :] = jnp.zeros((256 if dr == 0 else 64, H), F32)

    def grad_copy(i, e):
        dr, dc = SIDES[i]
        to = {"row": row + dr, "col": col + dc}
        if dc == 0:
            src, dst = gr_out.at[i, e], gr_in.at[i, e]
        elif dr == 0:
            src, dst = gc_out.at[i - 2, e], gc_in.at[i - 2, e]
        else:
            src, dst = gk_out.at[i - 4, e], gk_in.at[i - 4, e]
        return pltpu.make_async_remote_copy(
            src_ref=src, dst_ref=dst, send_sem=grad_send.at[i, e], recv_sem=grad_recv.at[i, e],
            device_id=to, device_id_type=MESH,
        )

    def hand_over(e):
        for i, (dr, dc) in enumerate(SIDES):
            rr = pl.ds(0 if dr < 0 else 320, 64)
            tile = 0 if dc < 0 else 3

            @pl.when(inside(dr, dc))
            def _():
                if dc == 0:
                    for c in (0, 1):
                        for j in (0, 1):
                            gr_out[i, e, c, :, pl.ds(j * H, H)] = grad[c, 1 + j, rr, :]
                elif dr == 0:
                    for c in (0, 1):
                        gc_out[i - 2, e, c] = fold(
                            (grad[c, tile, pl.ds(64, H), :], grad[c, tile, pl.ds(64 + H, H), :]), dc > 0
                        )
                else:
                    gk_out[i - 4, e] = fold((grad[0, tile, rr, :], grad[1, tile, rr, :]), dc > 0)
                grad_copy(i, e).start()
        for c in (0, 1):
            for j in (0, 1):
                at = pl.ds(j * H, H)
                stepped[e, c, :, at] = obj[e, c, :, at] - STEP * grad[c, 1 + j, pl.ds(64, N), :]

    def in_copy(slot, e):
        to, _ = peer(slot)
        return pltpu.make_async_remote_copy(
            src_ref=stepped.at[e, :, pl.ds(pl.multiple_of(32 * to, 32), 32), :],
            dst_ref=gathered.at[e, me],
            send_sem=in_send.at[slot - 1, e], recv_sem=in_recv.at[slot - 1, e],
            device_id={"energy": to}, device_id_type=MESH,
        )

    def finish(e):
        for i, (dr, dc) in enumerate(SIDES):
            rr = pl.ds(0 if dr > 0 else N - HALO, HALO)
            at = pl.ds(0 if dc > 0 else H, H)

            @pl.when(inside(-dr, -dc))
            def _():
                grad_copy(i, e).wait_recv()
                for c in (0, 1):
                    if dc == 0:
                        stepped[e, c, rr, :] -= STEP * gr_in[i, e, c]
                    elif dr == 0:
                        v = gc_in[i - 2, e, c]
                        m = low if dc > 0 else ~low
                        stepped[e, c, pl.ds(0, H), at] -= STEP * jnp.where(m, v, 0.0)
                        stepped[e, c, pl.ds(H, H), at] -= STEP * jnp.where(m, pltpu.roll(v, 64, 1), 0.0)
                    else:
                        v = gk_in[i - 4, e]
                        v = v if c == 0 else pltpu.roll(v, 64, 1)
                        stepped[e, c, rr, at] -= STEP * jnp.where(low64 if dc > 0 else ~low64, v, 0.0)
        for slot in (4, 5, 2, 6, 3, 7, 1):
            in_copy(slot, e).start()
        gathered[e, me] = stepped[e, :, pl.ds(pl.multiple_of(32 * me, 32), 32), :]

    mine = 128 * core

    def p_copy(step, e, i):
        index = (0, 1, 4, 5, 8)[step] + (i - 1 if i else 0)
        if step == 0:
            theirs = pl.ds(pl.multiple_of(128 * (1 - core), 128), 128)
            src, dst, to = pg.at[e, :, theirs, :], core_in.at[e], partner
        elif step == 1:
            r2 = lax.rem(row + i, rows)
            src = pg.at[e, :, pl.ds(pl.multiple_of(mine + 32 * r2, 32), 32), :]
            dst, to = row_in.at[e, i - 1], {"row": r2}
        elif step == 2:
            src = pg.at[e, :, pl.ds(pl.multiple_of(mine + 32 * row, 32), 32), :]
            dst, to = far_in.at[e], across
        elif step == 3:
            src = total.at[e, :, pl.ds(pl.multiple_of(mine + 32 * row, 32), 32), :]
            dst, to = src, {"row": lax.rem(row + i, rows)}
        else:
            src = total.at[e, :, pl.ds(pl.multiple_of(mine, 128), 128), :]
            dst, to = src, partner
        return pltpu.make_async_remote_copy(
            src_ref=src, dst_ref=dst, send_sem=p_send.at[e, index], recv_sem=p_recv.at[e, index],
            device_id=to, device_id_type=MESH,
        )

    def probe_step(step, e):
        chunk = pl.ds(pl.multiple_of(mine + 32 * row, 32), 32)
        if step == 0:
            p_copy(0, e, 0).start()
        elif step == 1:
            p_copy(0, e, 0).wait_recv()
            half = pl.ds(pl.multiple_of(mine, 128), 128)
            pg[e, :, half, :] += core_in[e]
            for i in (2, 1, 3):
                p_copy(1, e, i).start()
        elif step == 2:
            for i in (1, 2, 3):
                p_copy(1, e, i).wait_recv()
            pg[e, :, chunk, :] += row_in[e, 0] + row_in[e, 1] + row_in[e, 2]
            p_copy(2, e, 0).start()
        elif step == 3:
            p_copy(2, e, 0).wait_recv()
            total[e, :, chunk, :] = pg[e, :, chunk, :] + far_in[e]
            for i in (2, 1, 3):
                p_copy(3, e, i).start()
        else:
            for i in (1, 2, 3):
                p_copy(3, e, i).wait_recv()
            p_copy(4, e, 0).start()

    def front(k, e, buffers):
        return forward(
            k, offs[0, 0, 0, k], offs[0, 0, 1, k], ext, probe.at[:, e], amp.at[e, k], tab, order, *buffers
        )

    def rear(k, e, buffers):
        return backward(
            k, offs[0, 0, 0, k], offs[0, 0, 1, k], probe.at[:, e], grad, pg.at[e], tab, *buffers
        )

    def body(t, _):
        e, odd = lax.div(t, 2), lax.rem(t, 2)

        @pl.when((odd == 0) & (e > 1))
        def _():
            finish(e - 2)

        @pl.when(odd == 0)
        def _():
            assemble(e)

        last = jnp.maximum(lax.div(2 * t - 1, 4), 0)
        together(ORDER, rear(3 - 2 * odd, last, work_b), front(2 * odd, e, work_a))

        @pl.when((odd == 0) & (e > 0))
        def _():
            hand_over(e - 1)
            grad[...] = jnp.zeros_like(grad)
            probe_step(0, e - 1)

        @pl.when((odd == 1) & (e > 0))
        def _():
            probe_step(1, e - 1)

        @pl.when((odd == 1) & (e > 1))
        def _():
            probe_step(2, e - 2)

        together(ORDER, rear(2 * odd, e, work_a), front(2 * odd + 1, e, work_b))
        return 0

    lax.fori_loop(0, 8, body, 0)
    finish(2)
    together(ORDER, rear(3, 3, work_b))
    hand_over(3)
    probe_step(0, 3)
    probe_step(1, 3)
    probe_step(2, 2)
    finish(3)
    probe_step(3, 0)
    probe_step(3, 1)

    def half_product(g, half):
        x = gathered[pl.ds(2 * half, 2), :, :, pl.ds(8 * g, 8), :].reshape(N, N)
        hi, lo = split(x)
        k_hi, k_lo = kx[0, :, pl.ds(N * half, N)], kx[1, :, pl.ds(N * half, N)]
        return dot(
            jnp.concatenate([k_hi, k_lo, k_hi], axis=1), jnp.concatenate([hi, hi, lo], axis=0)
        )

    for e in (0, 1):
        for slot in range(1, 8):
            in_copy(slot, e).wait_recv()
    for g in range(4):
        acc[g] = half_product(g, 0)
    for e in (2, 3):
        for slot in range(1, 8):
            in_copy(slot, e).wait_recv()

    probe_step(2, 3)

    def out_copy(slot, g):
        to, _ = peer(slot)
        return pltpu.make_async_remote_copy(
            src_ref=coupled.at[to, :, :, pl.ds(8 * g, 8), :],
            dst_ref=returned.at[:, :, me, pl.ds(8 * g, 8), :],
            send_sem=out_send.at[slot - 1, g], recv_sem=out_recv.at[slot - 1, g],
            device_id={"energy": to}, device_id_type=MESH,
        )

    for g in range(4):
        out = acc[g] + half_product(g, 1)
        coupled[:, :, :, pl.ds(8 * g, 8), :] = out.reshape(8, 2, 4, 8, N)
        for slot in (4, 5, 2, 6, 3, 7, 1):
            out_copy(slot, g).start()
    returned[:, :, me] = coupled[me]
    for step, e in ((3, 2), (3, 3), (4, 0), (4, 1), (4, 2), (4, 3)):
        probe_step(step, e)
    rate = PROBE_STEP / (4 * rows * cols)
    for e in range(4):
        p_copy(4, e, 0).wait_recv()
        for c in (0, 1):
            new_probe[c, e] = probe[c, e] - rate * total[e, c]
    for e in range(4):
        for step in range(5):
            for i in ((0,) if step in (0, 2, 4) else (1, 2, 3)):
                p_copy(step, e, i).wait_send()
        for slot in range(1, 8):
            in_copy(slot, e).wait_send()
    for i, (dr, dc) in enumerate(SIDES):
        @pl.when(inside(dr, dc))
        def _():
            for e in range(4):
                halo_copy(i, e).wait_send()
                grad_copy(i, e).wait_send()
    for g in range(4):
        for slot in range(1, 8):
            out_copy(slot, g).wait_recv()
        for c in (0, 1):
            for e in range(4):
                for d in range(8):
                    at = pl.ds(32 * d + 8 * g, 8)
                    blended[c, e, at, :] = stepped[e, c, at, :] + returned[c, e, d, pl.ds(8 * g, 8), :]
    for g in range(4):
        for slot in range(1, 8):
            out_copy(slot, g).wait_send()


def local(object_field, probe_field, amplitudes, kk_kernel, offsets):
    tab, order = tables()
    vm = lambda *shape: pltpu.VMEM(shape, F32)
    vb = lambda *shape: pltpu.VMEM(shape, BF)
    dma = pltpu.SemaphoreType.DMA
    anywhere = pl.BlockSpec(memory_space=pl.ANY)
    return pl.pallas_call(
        kernel,
        in_specs=[
            pl.BlockSpec(memory_space=pltpu.SMEM), anywhere, anywhere, anywhere,
            pl.BlockSpec(memory_space=pltpu.VMEM), anywhere, anywhere,
        ],
        out_specs=[pl.BlockSpec(memory_space=pltpu.VMEM)] * 2,
        out_shape=[pltpu.VMEM(object_field.shape, F32), pltpu.VMEM(probe_field.shape, F32)],
        scratch_shapes=[
            vm(4, 2, N, N), vm(2, 4, N, N), vm(4, 4, N, N), vb(2, 2, 2, N, N), vb(N, N), vb(2, 512, 512),
            vm(2, 4, 2, 64, N), vm(2, 4, 2, H, H), vm(4, 4, 64, H), vm(2, 4, 2, H, H), vm(4, 4, 64, H),
            vm(2, 4, 2, 64, N), vm(2, 4, 2, H, H), vm(4, 4, 64, H),
            vm(2, 4, 2, 64, N), vm(2, 4, 2, H, H), vm(4, 4, 64, H),
            vm(2, 4, 384, H), vm(2, 4, 384, H), vm(4, 2, N, N), vm(4, 8, 2, 32, N), vm(4, 512, N),
            vm(8, 2, 4, 32, N), vm(2, 4, 8, 32, N),
            vm(4, 2, N, N), vm(4, 2, H, N), vm(4, 3, 2, 32, N), vm(4, 2, 32, N), vm(4, 2, N, N),
            dma((11,)), dma((8, 4)), dma((8, 4)), dma((8, 4)), dma((8, 4)),
            dma((7, 4)), dma((7, 4)), dma((7, 4)), dma((7, 4)), dma((4, 9)), dma((4, 9)),
        ] + 2 * [
            vm(2, N, N), vm(2, N, N), vb(N, 2 * N), vb(N, 2 * N), vb(2 * N, N), vb(2 * N, N),
            vb(N, 2 * N), vm(2, N, H), vm(2, 3, 320, H),
        ],
        compiler_params=pltpu.CompilerParams(
            collective_id=0, has_side_effects=True, vmem_limit_bytes=56 * 2**20
        ),
        name="gradient_step",
    )(
        jnp.swapaxes(offsets, 2, 3), object_field, probe_field, amplitudes, kk_kernel,
        jnp.asarray(tab), jnp.asarray(order),
    )


def solution(mesh):
    return jax.shard_map(
        local,
        mesh=mesh,
        in_specs=(
            P(None, "energy", "row", "col"),
            P(None, "energy", None, None),
            P("energy", "row", "col", None, None, None),
            P(),
            P("row", "col", None, None),
        ),
        out_specs=(P(None, "energy", "row", "col"), P(None, "energy", None, None)),
        check_vma=False,
    )
```

```python
import functools

import jax
import jax.numpy as jnp
import numpy as np
from jax import lax
from jax.experimental import pallas as pl
from jax.experimental.pallas import tpu as pltpu
from jax.sharding import PartitionSpec as P

H = 128
N = 256
HALO = 64
STEP = 0.25
PROBE_STEP = 0.5
FLOOR = 0.25
F32 = jnp.float32
BF = jnp.bfloat16
MESH = pl.DeviceIdType.MESH
SIDES = ((-1, 0), (1, 0), (0, -1), (0, 1), (-1, -1), (-1, 1), (1, -1), (1, 1))


def tables():
    n = np.arange(H)[:, None].astype(np.float64)
    k = np.arange(H)[None, :].astype(np.float64)
    out = []
    for odd in (0, 1):
        angle = -2.0 * np.pi * ((n * (2 * k + odd)) % N) / N
        re, im = np.cos(angle) / 16.0, np.sin(angle) / 16.0
        out.append(np.block([[re, im], [-im, re]]))
    right = np.stack(out)
    both = np.stack([right, np.swapaxes(right, 1, 2)])
    hi = both.astype(np.float32).astype(jnp.bfloat16)
    lo = (both - hi.astype(np.float64)).astype(np.float32).astype(jnp.bfloat16)
    order = np.zeros((N, N), np.float32)
    for lane in range(H):
        order[2 * lane, lane] = 1
        order[2 * lane + 1, H + lane] = 1
    return np.stack([hi, lo], axis=2), order.astype(jnp.bfloat16)


def split(x):
    hi = x.astype(BF)
    return hi, (x - hi.astype(F32)).astype(BF)


def dot(a, b):
    return jnp.dot(a, b, preferred_element_type=F32)


def times_table(q, tab, side, odd):
    hi, lo = tab[side, odd, 0], tab[side, odd, 1]
    return dot(
        jnp.concatenate([q[...], q[:, :N]], axis=1), jnp.concatenate([hi, hi, lo], axis=0)
    )


def table_times(tab, side, odd, q):
    hi, lo = tab[side, odd, 0], tab[side, odd, 1]
    return dot(
        jnp.concatenate([hi, hi, lo], axis=1), jnp.concatenate([q[...], q[:N, :]], axis=0)
    )


def forward(k, a, b, ext, probe, amp, tab, order, win, exi, ra, rb, la, lb, ap, asc, opad):
    base = lax.rem(k, 2)
    s = b + HALO - H * base
    rows_at = 64
    lane = lax.broadcasted_iota(jnp.int32, (rows_at, H), 1)
    keep = lane < H - s
    for rc in range(0, N, rows_at):
        rows = pl.ds(rc, rows_at)
        w = []
        for c in (0, 1):
            t = [pltpu.roll(ext[c, base + j, pl.ds(a + rc, rows_at), :], H - s, 1) for j in range(3)]
            w.append([jnp.where(keep, t[j], t[j + 1]) for j in (0, 1)])
        x = [[None, None], [None, None]]
        for j in (0, 1):
            cols = pl.ds(j * H, H)
            pr, pi = probe[0, rows, cols], probe[1, rows, cols]
            wr, wi = w[0][j], w[1][j]
            win[0, rows, cols] = wr
            win[1, rows, cols] = wi
            x[0][j] = pr * wr - pi * wi
            x[1][j] = pr * wi + pi * wr
            exi[0, rows, cols] = x[0][j]
            exi[1, rows, cols] = x[1][j]
        for c in (0, 1):
            for q, v in ((ra, x[c][0] + x[c][1]), (rb, x[c][0] - x[c][1])):
                hi, lo = split(v)
                q[rows, pl.ds(c * H, H)] = hi
                q[rows, pl.ds(N + c * H, H)] = lo
        hi, lo = split(amp[rows, :])
        ap[rows, pl.ds(0, N)] = hi
        ap[rows, pl.ds(N, N)] = lo
    yield
    y = [times_table(ra, tab, 0, 0), times_table(rb, tab, 0, 1)]
    amps = dot(ap[...], jnp.concatenate([order[...], order[...]], axis=0))
    yield
    for pc in (0, 1):
        cols = pl.ds(pc * H, H)
        for c in (0, 1):
            t = y[pc][:H, c * H:(c + 1) * H]
            u = y[pc][H:, c * H:(c + 1) * H]
            for q, v in ((la, t + u), (lb, t - u)):
                hi, lo = split(v)
                q[pl.ds(c * H, H), cols] = hi
                q[pl.ds(N + c * H, H), cols] = lo
    asc[0] = amps[:, :H]
    asc[1] = amps[:, H:]
    yield
    z = [table_times(tab, 1, 0, la), table_times(tab, 1, 1, lb)]
    yield
    for pr, q in ((0, la), (1, lb)):
        fr, fi = z[pr][:H], z[pr][H:]
        measured = jnp.concatenate([asc[j, pl.ds(pr, H, stride=2), :] for j in (0, 1)], axis=1)
        scale = measured * lax.rsqrt(jnp.maximum(fr * fr + fi * fi, FLOOR * FLOOR))
        for c, v in ((0, fr * scale), (1, fi * scale)):
            hi, lo = split(v)
            q[pl.ds(c * H, H), :] = hi
            q[pl.ds(N + c * H, H), :] = lo
    yield


def backward(k, a, b, probe, grad, pg, tab, win, exi, ra, rb, la, lb, ap, asc, opad):
    base = lax.rem(k, 2)
    s = b + HALO - H * base
    rows_at = 64
    lane = lax.broadcasted_iota(jnp.int32, (rows_at, H), 1)
    p, q = table_times(tab, 0, 0, la), table_times(tab, 0, 1, lb)
    yield
    for half, v in ((0, p + q), (1, p - q)):
        rows = pl.ds(half * H, H)
        for pc, dst in ((0, ra), (1, rb)):
            for c in (0, 1):
                hi, lo = split(v[c * H:(c + 1) * H, pc * H:(pc + 1) * H])
                dst[rows, pl.ds(c * H, H)] = hi
                dst[rows, pl.ds(N + c * H, H)] = lo
    yield
    p, q = times_table(ra, tab, 1, 0), times_table(rb, tab, 1, 1)
    yield
    back = (p + q, p - q)
    turned = lane >= s
    for rc in range(0, N, rows_at):
        rows = pl.ds(rc, rows_at)
        step = [[None] * 2, [None] * 2]
        for j in (0, 1):
            cols = pl.ds(j * H, H)
            dr = exi[0, rows, cols] - back[j][rc:rc + rows_at, :H]
            di = exi[1, rows, cols] - back[j][rc:rc + rows_at, H:]
            pr, pi = probe[0, rows, cols], probe[1, rows, cols]
            wr, wi = win[0, rows, cols], win[1, rows, cols]
            pg[0, rows, cols] += wr * dr + wi * di
            pg[1, rows, cols] += wr * di - wi * dr
            step[0][j] = pltpu.roll(pr * dr + pi * di, s, 1)
            step[1][j] = pltpu.roll(pr * di - pi * dr, s, 1)
        for c in (0, 1):
            at = pl.ds(32 + rc, rows_at)
            opad[c, 0, at, :] = jnp.where(turned, step[c][0], 0.0)
            opad[c, 1, at, :] = jnp.where(turned, step[c][1], step[c][0])
            opad[c, 2, at, :] = jnp.where(turned, 0.0, step[c][1])
    yield
    first = 96 * lax.div(k, 2)
    start = 32 - jnp.clip(a - first, 0, 32)
    for c in (0, 1):
        for j in range(3):
            for rc in range(0, 288, 32):
                at = pl.ds(pl.multiple_of(first + rc, 32), 32)
                grad[c, base + j, at, :] += opad[c, j, pl.ds(start + rc, 32), :]
    yield


ORDER = "frfrrffrrf"


def together(order, back, forth=None):
    for which in order:
        if which == "r":
            next(back)
        elif forth is not None:
            next(forth)


def expand_kernel(kk, kx):
    out_row = lax.broadcasted_iota(jnp.int32, (512, 32), 0)
    out_col = lax.broadcasted_iota(jnp.int32, (512, 32), 1)
    out_energy = 4 * (out_row >> 6) + ((out_row >> 3) & 3)
    in_row = lax.broadcasted_iota(jnp.int32, (32, 512), 0)
    in_col = lax.broadcasted_iota(jnp.int32, (32, 512), 1)
    in_energy = 4 * ((in_col >> 4) & 7) + (in_col >> 7)
    r = lax.broadcasted_iota(jnp.int32, (512, 512), 0)
    c = lax.broadcasted_iota(jnp.int32, (512, 512), 1)
    same = (r & 7) == (c & 7)
    one = lambda m: jnp.where(m, 1.0, 0.0).astype(BF)
    pick = [one((in_energy == in_row) & (((in_col >> 3) & 1) == b)) for b in (0, 1)]
    place = [one((out_energy == out_col) & (((out_row >> 5) & 1) == a)) for a in (0, 1)]
    parts = [[split(kk[a, b]) for b in (0, 1)] for a in (0, 1)]
    for which in (0, 1):
        total = None
        for a in (0, 1):
            row = dot(parts[a][0][which], pick[0]) + dot(parts[a][1][which], pick[1])
            term = dot(place[a], row.astype(BF))
            total = term if total is None else total + term
        kx[which] = jnp.where(same, total, 0.0).astype(BF)


def kernel(
    offs, obj_any, probe_any, amp_any, kk, tab_any, order_any,
    blended, new_probe,
    obj, probe, amp, tab, order, kx,
    halo_rows, halo_cols, halo_corners, cols_out, corners_out,
    gr_in, gc_in, gk_in, gr_out, gc_out, gk_out,
    ext, grad, stepped, gathered, acc, coupled, returned,
    pg, core_in, row_in, far_in, total,
    load_sem, halo_send, halo_recv, grad_send, grad_recv,
    in_send, in_recv, last_send, last_recv, out_send, out_recv, p_send, p_recv,
    *work,
):
    work_a, work_b = work[:9], work[9:]
    me = lax.axis_index("energy")
    row = lax.axis_index("row")
    col = lax.axis_index("col")
    rows, cols = lax.axis_size("row"), lax.axis_size("col")
    core = lax.rem(col, 2)
    partner = {"col": col + 1 - 2 * core}
    high = lax.div(col, 2)
    across = {"col": col + 2 - 4 * high}

    def peer(slot):
        dx, dy = slot // 2, slot % 2
        x, y = lax.div(me, 2), lax.rem(me, 2)
        y2 = y + dy * (1 - 2 * y)
        return lax.rem(x + dx, 4) * 2 + y2, lax.rem(x + 4 - dx, 4) * 2 + y2

    def inside(dr, dc):
        ok = None
        for d, at, n in ((dr, row, rows), (dc, col, cols)):
            if d:
                here = at > 0 if d < 0 else at < n - 1
                ok = here if ok is None else ok & here
        return ok

    loads = []
    for e in range(4):
        loads.append(pltpu.make_async_copy(obj_any.at[:, e], obj.at[e], load_sem.at[e]))
    loads.append(pltpu.make_async_copy(probe_any, probe, load_sem.at[4]))
    loads.append(pltpu.make_async_copy(tab_any, tab, load_sem.at[5]))
    loads.append(pltpu.make_async_copy(order_any, order, load_sem.at[6]))
    for e in range(4):
        loads.append(pltpu.make_async_copy(amp_any.at[e, 0, 0], amp.at[e], load_sem.at[7 + e]))
    for copy in loads:
        copy.start()

    barrier = pltpu.get_barrier_semaphore()

    def greet(device):
        pl.semaphore_signal(barrier, inc=1, device_id=device, device_id_type=MESH)

    for dr, dc in SIDES:
        @pl.when(inside(dr, dc))
        def _():
            greet({"row": row + dr, "col": col + dc})
    for slot in range(1, 8):
        greet({"energy": peer(slot)[0]})
    for d in range(1, 4):
        r2 = lax.rem(row + d, rows)

        @pl.when((r2 != row + 1) & (r2 != row - 1))
        def _():
            greet({"row": r2})
    greet(across)
    near_rows = jnp.where(row > 0, 1, 0) + jnp.where(row < rows - 1, 1, 0)
    near_cols = jnp.where(col > 0, 1, 0) + jnp.where(col < cols - 1, 1, 0)
    pl.semaphore_wait(barrier, 11 + near_cols + near_rows * near_cols)

    lane = lax.broadcasted_iota(jnp.int32, (H, H), 1)
    low = lane < 64
    lane64 = lax.broadcasted_iota(jnp.int32, (64, H), 1)
    low64 = lane64 < 64

    def fold(t, keep_low):
        first, second = t
        n = first.shape[0]
        m = low if n == H else low64
        return jnp.where(m if keep_low else ~m, first, pltpu.roll(second, 64, 1))

    def halo_copy(i, e):
        dr, dc = SIDES[i]
        to = {"row": row + dr, "col": col + dc}
        if dc == 0:
            src, dst = obj.at[e, :, pl.ds(0 if dr < 0 else N - HALO, HALO), :], halo_rows.at[i, e]
        elif dr == 0:
            src, dst = cols_out.at[i - 2, e], halo_cols.at[i - 2, e]
        else:
            src, dst = corners_out.at[i - 4, e], halo_corners.at[i - 4, e]
        return pltpu.make_async_remote_copy(
            src_ref=src, dst_ref=dst, send_sem=halo_send.at[i, e], recv_sem=halo_recv.at[i, e],
            device_id=to, device_id_type=MESH,
        )

    for e in range(4):
        loads[e].wait()
        for i, dc in ((2, -1), (3, 1)):
            at = pl.ds(0 if dc < 0 else H, H)
            for c in (0, 1):
                cols_out[i - 2, e, c] = fold((obj[e, c, :H, at], obj[e, c, H:, at]), dc < 0)
        for i in range(4, 8):
            dr, dc = SIDES[i]
            at = pl.ds(0 if dc < 0 else H, H)
            rr = pl.ds(0 if dr < 0 else N - HALO, HALO)
            corners_out[i - 4, e] = fold((obj[e, 0, rr, at], obj[e, 1, rr, at]), dc < 0)
        for i, (dr, dc) in enumerate(SIDES):
            @pl.when(inside(dr, dc))
            def _():
                halo_copy(i, e).start()

    expand_kernel(kk, kx)
    for buffers in (work_a, work_b):
        opad = buffers[8]
        opad[:, :, :32, :] = jnp.zeros((2, 3, 32, H), F32)
        opad[:, :, 288:, :] = jnp.zeros((2, 3, 32, H), F32)
    for part in (0, 1, 4, 5):
        work_b[part][...] = jnp.zeros_like(work_b[part])
    grad[...] = jnp.zeros_like(grad)
    loads[4].wait()
    loads[5].wait()
    loads[6].wait()
    pg[...] = jnp.zeros_like(pg)

    def assemble(e):
        pltpu.make_async_copy(amp_any.at[e, 0, 0], amp.at[e], load_sem.at[7 + e]).wait()
        for c in (0, 1):
            for j in (0, 1):
                ext[c, 1 + j, pl.ds(64, N), :] = obj[e, c, :, pl.ds(j * H, H)]
        for i, (dr, dc) in enumerate(SIDES):
            rr = pl.ds(64, N) if dr == 0 else pl.ds(0 if dr > 0 else 320, 64)
            tile = 0 if dc > 0 else 3

            @pl.when(inside(-dr, -dc))
            def _():
                halo_copy(i, e).wait_recv()
                for c in (0, 1):
                    if dc == 0:
                        for j in (0, 1):
                            ext[c, 1 + j, rr, :] = halo_rows[i, e, c, :, pl.ds(j * H, H)]
                    elif dr == 0:
                        v = halo_cols[i - 2, e, c]
                        ext[c, tile, pl.ds(64, H), :] = v
                        ext[c, tile, pl.ds(64 + H, H), :] = pltpu.roll(v, 64, 1)
                    else:
                        v = halo_corners[i - 4, e]
                        ext[c, tile, rr, :] = v if c == 0 else pltpu.roll(v, 64, 1)

            @pl.when(jnp.logical_not(inside(-dr, -dc)))
            def _():
                for c in (0, 1):
                    for t in ((1, 2) if dc == 0 else (tile,)):
                        ext[c, t, rr, :] = jnp.zeros((256 if dr == 0 else 64, H), F32)

    def grad_copy(i, e):
        dr, dc = SIDES[i]
        to = {"row": row + dr, "col": col + dc}
        if dc == 0:
            src, dst = gr_out.at[i, e], gr_in.at[i, e]
        elif dr == 0:
            src, dst = gc_out.at[i - 2, e], gc_in.at[i - 2, e]
        else:
            src, dst = gk_out.at[i - 4, e], gk_in.at[i - 4, e]
        return pltpu.make_async_remote_copy(
            src_ref=src, dst_ref=dst, send_sem=grad_send.at[i, e], recv_sem=grad_recv.at[i, e],
            device_id=to, device_id_type=MESH,
        )

    def hand_over(e):
        for i, (dr, dc) in enumerate(SIDES):
            rr = pl.ds(0 if dr < 0 else 320, 64)
            tile = 0 if dc < 0 else 3

            @pl.when(inside(dr, dc))
            def _():
                if dc == 0:
                    for c in (0, 1):
                        for j in (0, 1):
                            gr_out[i, e, c, :, pl.ds(j * H, H)] = grad[c, 1 + j, rr, :]
                elif dr == 0:
                    for c in (0, 1):
                        gc_out[i - 2, e, c] = fold(
                            (grad[c, tile, pl.ds(64, H), :], grad[c, tile, pl.ds(64 + H, H), :]), dc > 0
                        )
                else:
                    gk_out[i - 4, e] = fold((grad[0, tile, rr, :], grad[1, tile, rr, :]), dc > 0)
                grad_copy(i, e).start()
        for c in (0, 1):
            for j in (0, 1):
                at = pl.ds(j * H, H)
                stepped[e, c, :, at] = obj[e, c, :, at] - STEP * grad[c, 1 + j, pl.ds(64, N), :]

    def in_copy(slot, e):
        to, _ = peer(slot)
        return pltpu.make_async_remote_copy(
            src_ref=stepped.at[e, :, pl.ds(pl.multiple_of(32 * to, 32), 32), :],
            dst_ref=gathered.at[e, me],
            send_sem=in_send.at[slot - 1, e], recv_sem=in_recv.at[slot - 1, e],
            device_id={"energy": to}, device_id_type=MESH,
        )

    def last_copy(slot, g):
        to, _ = peer(slot)
        return pltpu.make_async_remote_copy(
            src_ref=stepped.at[3, :, pl.ds(pl.multiple_of(32 * to + 8 * g, 8), 8), :],
            dst_ref=gathered.at[3, me, :, pl.ds(8 * g, 8), :],
            send_sem=last_send.at[slot - 1, g], recv_sem=last_recv.at[slot - 1, g],
            device_id={"energy": to}, device_id_type=MESH,
        )

    def receive_grad(e, sides):
        for i in sides:
            dr, dc = SIDES[i]
            rr = pl.ds(0 if dr > 0 else N - HALO, HALO)
            at = pl.ds(0 if dc > 0 else H, H)

            @pl.when(inside(-dr, -dc))
            def _():
                grad_copy(i, e).wait_recv()
                for c in (0, 1):
                    if dc == 0:
                        stepped[e, c, rr, :] -= STEP * gr_in[i, e, c]
                    elif dr == 0:
                        v = gc_in[i - 2, e, c]
                        m = low if dc > 0 else ~low
                        stepped[e, c, pl.ds(0, H), at] -= STEP * jnp.where(m, v, 0.0)
                        stepped[e, c, pl.ds(H, H), at] -= STEP * jnp.where(m, pltpu.roll(v, 64, 1), 0.0)
                    else:
                        v = gk_in[i - 4, e]
                        v = v if c == 0 else pltpu.roll(v, 64, 1)
                        stepped[e, c, rr, at] -= STEP * jnp.where(low64 if dc > 0 else ~low64, v, 0.0)

    def finish(e):
        receive_grad(e, range(8))
        for slot in (4, 5, 2, 6, 3, 7, 1):
            in_copy(slot, e).start()
        gathered[e, me] = stepped[e, :, pl.ds(pl.multiple_of(32 * me, 32), 32), :]

    mine = 128 * core

    def p_copy(step, e, i):
        index = (0, 1, 4, 5, 8)[step] + (i - 1 if i else 0)
        if step == 0:
            theirs = pl.ds(pl.multiple_of(128 * (1 - core), 128), 128)
            src, dst, to = pg.at[e, :, theirs, :], core_in.at[e], partner
        elif step == 1:
            r2 = lax.rem(row + i, rows)
            src = pg.at[e, :, pl.ds(pl.multiple_of(mine + 32 * r2, 32), 32), :]
            dst, to = row_in.at[e, i - 1], {"row": r2}
        elif step == 2:
            src = pg.at[e, :, pl.ds(pl.multiple_of(mine + 32 * row, 32), 32), :]
            dst, to = far_in.at[e], across
        elif step == 3:
            src = total.at[e, :, pl.ds(pl.multiple_of(mine + 32 * row, 32), 32), :]
            dst, to = src, {"row": lax.rem(row + i, rows)}
        else:
            src = total.at[e, :, pl.ds(pl.multiple_of(mine, 128), 128), :]
            dst, to = src, partner
        return pltpu.make_async_remote_copy(
            src_ref=src, dst_ref=dst, send_sem=p_send.at[e, index], recv_sem=p_recv.at[e, index],
            device_id=to, device_id_type=MESH,
        )

    def probe_step(step, e):
        chunk = pl.ds(pl.multiple_of(mine + 32 * row, 32), 32)
        if step == 0:
            p_copy(0, e, 0).start()
        elif step == 1:
            p_copy(0, e, 0).wait_recv()
            half = pl.ds(pl.multiple_of(mine, 128), 128)
            pg[e, :, half, :] += core_in[e]
            for i in (2, 1, 3):
                p_copy(1, e, i).start()
        elif step == 2:
            for i in (1, 2, 3):
                p_copy(1, e, i).wait_recv()
            pg[e, :, chunk, :] += row_in[e, 0] + row_in[e, 1] + row_in[e, 2]
            p_copy(2, e, 0).start()
        elif step == 3:
            p_copy(2, e, 0).wait_recv()
            total[e, :, chunk, :] = pg[e, :, chunk, :] + far_in[e]
            for i in (2, 1, 3):
                p_copy(3, e, i).start()
        else:
            for i in (1, 2, 3):
                p_copy(3, e, i).wait_recv()
            p_copy(4, e, 0).start()

    def front(k, e, buffers):
        return forward(
            k, offs[0, 0, 0, k], offs[0, 0, 1, k], ext, probe.at[:, e], amp.at[e, k], tab, order, *buffers
        )

    def rear(k, e, buffers):
        return backward(
            k, offs[0, 0, 0, k], offs[0, 0, 1, k], probe.at[:, e], grad, pg.at[e], tab, *buffers
        )

    def body(t, _):
        e, odd = lax.div(t, 2), lax.rem(t, 2)

        @pl.when(odd == 0)
        def _():
            assemble(e)

        last = jnp.maximum(lax.div(2 * t - 1, 4), 0)
        together(ORDER, rear(3 - 2 * odd, last, work_b), front(2 * odd, e, work_a))

        @pl.when((odd == 0) & (e > 0))
        def _():
            hand_over(e - 1)
            grad[...] = jnp.zeros_like(grad)

        @pl.when((odd == 0) & (e > 1))
        def _():
            finish(e - 2)

        for step in range(3):
            @pl.when((odd == 0) & (e > step))
            def _():
                probe_step(step, e - 1 - step)

        together(ORDER, rear(2 * odd, e, work_a), front(2 * odd + 1, e, work_b))
        return 0

    lax.fori_loop(0, 8, body, 0)
    together(ORDER, rear(3, 3, work_b))
    hand_over(3)
    finish(2)
    for step in range(3):
        probe_step(step, 3 - step)
    receive_grad(3, (2, 3))
    for first in (True, False):
        if not first:
            receive_grad(3, (0, 1, 4, 5, 6, 7))
        for g in range(4):
            for slot in (4, 5, 2, 6, 3, 7, 1):
                to = peer(slot)[0]
                inner = (to >= 2) & (to <= 5)

                @pl.when(inner if first else jnp.logical_not(inner))
                def _():
                    last_copy(slot, g).start()
    gathered[3, me] = stepped[3, :, pl.ds(pl.multiple_of(32 * me, 32), 32), :]
    for step in (1, 2):
        probe_step(step, 4 - step)

    def half_product(g, half):
        x = gathered[pl.ds(2 * half, 2), :, :, pl.ds(8 * g, 8), :].reshape(N, N)
        hi, lo = split(x)
        k_hi, k_lo = kx[0, :, pl.ds(N * half, N)], kx[1, :, pl.ds(N * half, N)]
        return dot(
            jnp.concatenate([k_hi, k_lo, k_hi], axis=1), jnp.concatenate([hi, hi, lo], axis=0)
        )

    for e in (0, 1):
        for slot in range(1, 8):
            in_copy(slot, e).wait_recv()
    for g in range(4):
        acc[g] = half_product(g, 0)
    for slot in range(1, 8):
        in_copy(slot, 2).wait_recv()

    def out_copy(slot, g):
        to, _ = peer(slot)
        return pltpu.make_async_remote_copy(
            src_ref=coupled.at[to, :, :, pl.ds(8 * g, 8), :],
            dst_ref=returned.at[:, :, me, pl.ds(8 * g, 8), :],
            send_sem=out_send.at[slot - 1, g], recv_sem=out_recv.at[slot - 1, g],
            device_id={"energy": to}, device_id_type=MESH,
        )

    for g in range(4):
        for slot in range(1, 8):
            last_copy(slot, g).wait_recv()
        if g == 1:
            probe_step(2, 3)
        out = acc[g] + half_product(g, 1)
        coupled[:, :, :, pl.ds(8 * g, 8), :] = out.reshape(8, 2, 4, 8, N)
        for slot in (4, 5, 2, 6, 3, 7, 1):
            out_copy(slot, g).start()
    returned[:, :, me] = coupled[me]
    for step in (3, 4):
        for e in range(4):
            probe_step(step, e)
    rate = PROBE_STEP / (4 * rows * cols)
    for e in range(4):
        p_copy(4, e, 0).wait_recv()
        for c in (0, 1):
            new_probe[c, e] = probe[c, e] - rate * total[e, c]
    for e in range(4):
        for step in range(5):
            for i in ((0,) if step in (0, 2, 4) else (1, 2, 3)):
                p_copy(step, e, i).wait_send()
        for slot in range(1, 8):
            if e < 3:
                in_copy(slot, e).wait_send()
            last_copy(slot, e).wait_send()
    for i, (dr, dc) in enumerate(SIDES):
        @pl.when(inside(dr, dc))
        def _():
            for e in range(4):
                halo_copy(i, e).wait_send()
                grad_copy(i, e).wait_send()
    for g in range(4):
        for slot in range(1, 8):
            out_copy(slot, g).wait_recv()
        for c in (0, 1):
            for e in range(4):
                for d in range(8):
                    at = pl.ds(32 * d + 8 * g, 8)
                    blended[c, e, at, :] = stepped[e, c, at, :] + returned[c, e, d, pl.ds(8 * g, 8), :]
    for g in range(4):
        for slot in range(1, 8):
            out_copy(slot, g).wait_send()


def local(object_field, probe_field, amplitudes, kk_kernel, offsets):
    tab, order = tables()
    vm = lambda *shape: pltpu.VMEM(shape, F32)
    vb = lambda *shape: pltpu.VMEM(shape, BF)
    dma = pltpu.SemaphoreType.DMA
    anywhere = pl.BlockSpec(memory_space=pl.ANY)
    return pl.pallas_call(
        kernel,
        in_specs=[
            pl.BlockSpec(memory_space=pltpu.SMEM), anywhere, anywhere, anywhere,
            pl.BlockSpec(memory_space=pltpu.VMEM), anywhere, anywhere,
        ],
        out_specs=[pl.BlockSpec(memory_space=pltpu.VMEM)] * 2,
        out_shape=[pltpu.VMEM(object_field.shape, F32), pltpu.VMEM(probe_field.shape, F32)],
        scratch_shapes=[
            vm(4, 2, N, N), vm(2, 4, N, N), vm(4, 4, N, N), vb(2, 2, 2, N, N), vb(N, N), vb(2, 512, 512),
            vm(2, 4, 2, 64, N), vm(2, 4, 2, H, H), vm(4, 4, 64, H), vm(2, 4, 2, H, H), vm(4, 4, 64, H),
            vm(2, 4, 2, 64, N), vm(2, 4, 2, H, H), vm(4, 4, 64, H),
            vm(2, 4, 2, 64, N), vm(2, 4, 2, H, H), vm(4, 4, 64, H),
            vm(2, 4, 384, H), vm(2, 4, 384, H), vm(4, 2, N, N), vm(4, 8, 2, 32, N), vm(4, 512, N),
            vm(8, 2, 4, 32, N), vm(2, 4, 8, 32, N),
            vm(4, 2, N, N), vm(4, 2, H, N), vm(4, 3, 2, 32, N), vm(4, 2, 32, N), vm(4, 2, N, N),
            dma((11,)), dma((8, 4)), dma((8, 4)), dma((8, 4)), dma((8, 4)),
            dma((7, 3)), dma((7, 3)), dma((7, 4)), dma((7, 4)), dma((7, 4)), dma((7, 4)), dma((4, 9)), dma((4, 9)),
        ] + 2 * [
            vm(2, N, N), vm(2, N, N), vb(N, 2 * N), vb(N, 2 * N), vb(2 * N, N), vb(2 * N, N),
            vb(N, 2 * N), vm(2, N, H), vm(2, 3, 320, H),
        ],
        compiler_params=pltpu.CompilerParams(
            collective_id=0, has_side_effects=True, vmem_limit_bytes=56 * 2**20
        ),
        name="gradient_step",
    )(
        jnp.swapaxes(offsets, 2, 3), object_field, probe_field, amplitudes, kk_kernel,
        jnp.asarray(tab), jnp.asarray(order),
    )


def solution(mesh):
    return jax.shard_map(
        local,
        mesh=mesh,
        in_specs=(
            P(None, "energy", "row", "col"),
            P(None, "energy", None, None),
            P("energy", "row", "col", None, None, None),
            P(),
            P("row", "col", None, None),
        ),
        out_specs=(P(None, "energy", "row", "col"), P(None, "energy", None, None)),
        check_vma=False,
    )
```
